128 devices in a mesh: rep: 4 (over x), shard: 32 (over z, y, core).
Axes of the slice: x: 4, y: 4, z: 4, core: 2. Of those that a mesh axis runs over, the one named last changes fastest.
Arguments:
- attention_grad: bfloat16 [4, 8, 768, 768], P('rep', None, 'shard'), may hold values from -45 to 45
- dense_grad: bfloat16 [4, 2, 3072, 768], P('rep', None, 'shard'), may hold values from -45 to 45
- embedding_grad: bfloat16 [4, 8192, 768], P('rep', 'shard'), may hold values from -45 to 45
- attention_error: float32 [4, 8, 768, 768], P('rep', None, 'shard'), may hold values from -4 to 4
- dense_error: float32 [4, 2, 3072, 768], P('rep', None, 'shard'), may hold values from -4 to 4
- embedding_error: float32 [4, 8192, 768], P('rep', 'shard'), may hold values from -4 to 4
- attention_weight: float32 [8, 768, 768], P(None, 'shard'), may hold values from -0.21875 to 0.21875
- dense_weight: float32 [2, 3072, 768], P(None, 'shard'), may hold values from -0.21875 to 0.21875
- embedding_weight: float32 [8192, 768], P('shard'), may hold values from -0.21875 to 0.21875
- attention_momentum: float32 [8, 768, 768], P(None, 'shard'), may hold values from -1.5 to 1.5
- dense_momentum: float32 [2, 3072, 768], P(None, 'shard'), may hold values from -1.5 to 1.5
- embedding_momentum: float32 [8192, 768], P('shard'), may hold values from -1.5 to 1.5
- warm_start: float32 [11, 32, 768], replicated, may hold values from -0.21875 to 0.21875
- norm_scale: float32 [3, 768], P(None, 'shard'), may hold values from 0.5 to 1.5
- norm_momentum: float32 [3, 768], P(None, 'shard'), may hold values from -1.5 to 1.5
- norm_grad: float32 [4, 3, 768], P('rep', None, 'shard'), may hold values from -6 to 6
Outputs:
- attention_updated: float32 [8, 768, 768], P(None, 'shard')
- dense_updated: float32 [2, 3072, 768], P(None, 'shard')
- embedding_updated: float32 [8192, 768], P('shard')
- attention_copy: bfloat16 [8, 768, 768], P(None, 'shard')
- dense_copy: bfloat16 [2, 3072, 768], P(None, 'shard')
- embedding_copy: bfloat16 [8192, 768], P('shard')
- attention_residue: float32 [4, 8, 768, 768], P('rep', None, 'shard')
- dense_residue: float32 [4, 2, 3072, 768], P('rep', None, 'shard')
- embedding_residue: float32 [4, 8192, 768], P('rep', 'shard')
- attention_velocity: float32 [8, 768, 768], P(None, 'shard')
- dense_velocity: float32 [2, 3072, 768], P(None, 'shard')
- embedding_velocity: float32 [8192, 768], P('shard')
- next_start: float32 [11, 32, 768], replicated
- norm_updated: float32 [3, 768], P(None, 'shard')
- norm_velocity: float32 [3, 768], P(None, 'shard')
The draws below stay inside these ranges and needn't reach their ends.
All inputs are finite; a program needn't handle non-finite values.
Results may differ from the reference program's by a relative error of at most 0.001.
Values sent between devices are 32-bit elements; how exact they have to be, the bound alone decides.
A program may use at most 64 MiB of HBM per device.

```python
import math
import jax
import jax.numpy as jnp
from jax import lax

D = 768
FF = 3072
RANK = 32
EMB = 8192
N_REP = 4


def scaled_draw(key, shape):
    keys = jax.random.split(key, 3)
    rows = shape[-2]
    row_index = jnp.arange(rows, dtype=jnp.float32).reshape(rows, 1)
    trend = jnp.exp(math.log(3.0) * row_index / rows)
    row_scale = jnp.exp(jax.random.uniform(keys[1], shape[:-1] + (1,), jnp.float32, 0.0, math.log(10.0)))
    column_scale = jnp.exp(jax.random.uniform(keys[2], (shape[-1],), jnp.float32, 0.0, math.log(10.0)))
    values = 0.05 * jax.random.truncated_normal(keys[0], -3.0, 3.0, shape, jnp.float32)
    return (values * row_scale * trend * column_scale).astype(jnp.bfloat16)


def draw_attention_grad(key, part):
    return scaled_draw(jax.random.fold_in(key, 11), (N_REP, 8, D, D))


def draw_dense_grad(key, part):
    return scaled_draw(jax.random.fold_in(key, 12), (N_REP, 2, FF, D))


def draw_embedding_grad(key, part):
    return scaled_draw(jax.random.fold_in(key, 13), (N_REP, EMB, D))


def levels(key, shape, cuts, least, high):
    def one(dim, parts):
        heights = jax.random.uniform(jax.random.fold_in(jax.random.fold_in(key, 6), dim), (parts,), jnp.float32, least / len(cuts), high / len(cuts))
        return jnp.repeat(jnp.exp(heights), shape[dim] // parts).reshape((-1,) + (1,) * (len(shape) - dim - 1))

    gain = one(*cuts[0])
    for cut in cuts[1:]:
        gain = gain * one(*cut)
    return gain


def normal_values(key, dims, spread, bound, cuts=(), kind=jnp.bfloat16):
    drawn = jax.random.normal(key, dims, jnp.float32) * spread
    if len(cuts) > 0:
        drawn = levels(key, dims, cuts, -0.22, 0.18) * drawn
    return jnp.clip(drawn, min=-bound, max=bound).astype(kind)


def setup_inputs(seed: int = 0) -> dict:
    seeds = jax.random.split(jax.random.key(seed), 17)
    return {
        "attention_grad": draw_attention_grad(jax.random.fold_in(seeds[16], 71), 0),
        "dense_grad": draw_dense_grad(jax.random.fold_in(seeds[16], 71), 0),
        "embedding_grad": draw_embedding_grad(jax.random.fold_in(seeds[16], 71), 0),
        "attention_error": normal_values(seeds[3], (N_REP, 8, D, D), 0.3, 4.0, ((0, 4), (2, 32)), jnp.float32),
        "dense_error": normal_values(seeds[4], (N_REP, 2, FF, D), 0.3, 4.0, ((0, 4), (2, 32)), jnp.float32),
        "embedding_error": normal_values(seeds[5], (N_REP, EMB, D), 0.3, 4.0, ((0, 4), (1, 32)), jnp.float32),
        "attention_weight": normal_values(seeds[6], (8, D, D), D ** -0.5, 0.21875, ((1, 32),), jnp.float32),
        "dense_weight": normal_values(seeds[7], (2, FF, D), D ** -0.5, 0.21875, ((1, 32),), jnp.float32),
        "embedding_weight": normal_values(seeds[8], (EMB, D), D ** -0.5, 0.21875, ((0, 32),), jnp.float32),
        "attention_momentum": normal_values(seeds[9], (8, D, D), 0.1, 1.5, ((1, 32),), jnp.float32),
        "dense_momentum": normal_values(seeds[10], (2, FF, D), 0.1, 1.5, ((1, 32),), jnp.float32),
        "embedding_momentum": normal_values(seeds[11], (EMB, D), 0.1, 1.5, ((0, 32),), jnp.float32),
        "warm_start": normal_values(seeds[12], (11, RANK, D), D ** -0.5, 0.21875, (), jnp.float32),
        "norm_scale": jnp.clip(1.0 + 0.1 * jax.random.normal(seeds[13], (3, D), jnp.float32), 0.5, 1.5),
        "norm_momentum": normal_values(seeds[14], (3, D), 0.1, 1.5, ((1, 32),), jnp.float32),
        "norm_grad": normal_values(seeds[15], (N_REP, 3, D), 1.0, 6.0, ((0, 4), (2, 32)), jnp.float32),
    }


def invert(grams):
    factor = jnp.linalg.cholesky(grams)
    identity = jnp.broadcast_to(jnp.eye(grams.shape[-1], dtype=grams.dtype), grams.shape)
    return lax.linalg.triangular_solve(factor, identity, left_side=True, lower=True)

def finish(merged, approx, weight, momentum):
    velocity = 0.9 * momentum + approx
    updated = weight - 0.05 * velocity
    return (updated, updated.astype(jnp.bfloat16), merged - approx[None], velocity)

def reference(attention_grad, dense_grad, embedding_grad, attention_error, dense_error, embedding_error, attention_weight, dense_weight, embedding_weight, attention_momentum, dense_momentum, embedding_momentum, warm_start, norm_scale, norm_momentum, norm_grad):
    highest = lax.Precision.HIGHEST
    replicas = attention_grad.shape[0]
    merged_attention = attention_grad.astype(jnp.float32) + attention_error
    merged_dense = dense_grad.astype(jnp.float32) + dense_error
    merged_embedding = embedding_grad.astype(jnp.float32) + embedding_error
    proj_attention = jnp.einsum('nmrc,mkc->mkr', merged_attention, warm_start[:8], precision=highest) / replicas
    proj_dense = jnp.einsum('nmrc,mkc->mkr', merged_dense, warm_start[8:10], precision=highest) / replicas
    proj_embedding = jnp.einsum('nrc,kc->kr', merged_embedding, warm_start[10], precision=highest) / replicas
    grams = jnp.concatenate([jnp.einsum('mkr,mjr->mkj', proj_attention, proj_attention, precision=highest), jnp.einsum('mkr,mjr->mkj', proj_dense, proj_dense, precision=highest), jnp.einsum('kr,jr->kj', proj_embedding, proj_embedding, precision=highest)[None]], 0)
    inverse = invert(grams)
    ortho_attention = jnp.einsum('mjk,mkr->mjr', inverse[:8], proj_attention, precision=highest)
    ortho_dense = jnp.einsum('mjk,mkr->mjr', inverse[8:10], proj_dense, precision=highest)
    ortho_embedding = jnp.einsum('jk,kr->jr', inverse[10], proj_embedding, precision=highest)
    right_attention = jnp.einsum('mkr,nmrc->mkc', ortho_attention, merged_attention, precision=highest) / replicas
    right_dense = jnp.einsum('mkr,nmrc->mkc', ortho_dense, merged_dense, precision=highest) / replicas
    right_embedding = jnp.einsum('kr,nrc->kc', ortho_embedding, merged_embedding, precision=highest) / replicas
    next_start = jnp.concatenate([right_attention, right_dense, right_embedding[None]], 0)
    approx_attention = jnp.einsum('mkr,mkc->mrc', ortho_attention, right_attention, precision=highest)
    approx_dense = jnp.einsum('mkr,mkc->mrc', ortho_dense, right_dense, precision=highest)
    approx_embedding = jnp.einsum('kr,kc->rc', ortho_embedding, right_embedding, precision=highest)
    a_upd, a_copy, a_res, a_vel = finish(merged_attention, approx_attention, attention_weight, attention_momentum)
    d_upd, d_copy, d_res, d_vel = finish(merged_dense, approx_dense, dense_weight, dense_momentum)
    e_upd, e_copy, e_res, e_vel = finish(merged_embedding, approx_embedding, embedding_weight, embedding_momentum)
    norm_velocity = 0.9 * norm_momentum + jnp.sum(norm_grad, axis=0) / replicas
    norm_updated = norm_scale - 0.05 * norm_velocity
    return (a_upd, d_upd, e_upd, a_copy, d_copy, e_copy, a_res, d_res, e_res, a_vel, d_vel, e_vel, next_start, norm_updated, norm_velocity)
```

```python
import jax
import jax.numpy as jnp
from jax import lax
from jax.experimental import pallas as pl
from jax.experimental.pallas import tpu as pltpu
from jax.sharding import PartitionSpec as P

MESH = pl.DeviceIdType.MESH
F32, BF16 = jnp.float32, jnp.bfloat16
D = 768
HALF = 384
RANK = 32
NMAT = 11
LEFT = NMAT * RANK
ROWS = 640
AD_ROWS = 384
AD_LEFT = 10 * RANK
NT = (((1,), (1,)), ((), ()))
NN = (((1,), (0,)), ((), ()))
TN = (((0,), (0,)), ((), ()))


def split(x):
    hi = x.astype(BF16)
    return hi, (x - hi.astype(F32)).astype(BF16)


def dot(a, b, dims):
    return lax.dot_general(a, b, dims, preferred_element_type=F32)


def dot3(a, b, dims):
    (ah, al), (bh, bl) = a, b
    return dot(ah, bh, dims) + (dot(al, bh, dims) + dot(ah, bl, dims))


def exact(a, b, dims):
    return lax.dot_general(a, b, dims, preferred_element_type=F32, precision=lax.Precision.HIGHEST)


def row_mask(lefts, rows):
    m = lax.broadcasted_iota(jnp.int32, (lefts, rows), 0) // RANK
    r = lax.broadcasted_iota(jnp.int32, (lefts, rows), 1)
    low = jnp.where(m < 8, 24 * m, jnp.where(m < 10, 96 * m - 576, AD_ROWS))
    high = low + jnp.where(m < 8, 24, jnp.where(m < 10, 96, 256))
    return (r >= low) & (r < high)


def fold(x, blocks):
    total = x[:RANK]
    for m in range(1, blocks):
        total = total + x[m * RANK : (m + 1) * RANK]
    return total


def position():
    x, s = lax.axis_index("rep"), lax.axis_index("shard")
    return x, s // 2, s % 2


def device(x, plane, core):
    return (x, plane * 2 + core)


def exchange_kernel(
    ag_hbm, dg_hbm, eg_hbm, ae_hbm, de_hbm, ee_hbm, warm_hbm, norm_ref,
    right_hbm, left_hbm, norm_out,
    ag, dg, eg, ae, de, ee, warm, merged_hi, merged_lo,
    left_a, left_b, left_sum, other, own, sibling, slots, right, norm_slots,
    in_sem, left_send, left_recv, core_send, core_recv, rs_send, rs_recv,
    ag_send, ag_recv, half_send, half_recv, norm_send, norm_recv, out_sem,
):
    x, plane, core = position()
    chip = x * 16 + plane
    here = (plane * 11) % 16
    owner = here < NMAT

    barrier = pltpu.get_barrier_semaphore()
    pl.semaphore_signal(barrier, inc=1, device_id=device(x, plane, 1 - core), device_id_type=MESH)
    for d in range(1, 4):
        pl.semaphore_signal(barrier, inc=1, device_id=device((x + d) % 4, plane, core), device_id_type=MESH)

    def greet(i, carry):
        pl.semaphore_signal(barrier, inc=1, device_id=device(x, (plane + i) % 16, core), device_id_type=MESH)
        return carry

    lax.fori_loop(1, 16, greet, 0)

    loads = [
        pltpu.make_async_copy(a, b, in_sem.at[i])
        for i, (a, b) in enumerate(
            [(warm_hbm, warm), (ag_hbm, ag), (ae_hbm, ae), (dg_hbm, dg), (de_hbm, de), (eg_hbm, eg), (ee_hbm, ee)]
        )
    ]
    for copy in loads:
        copy.start()

    def put(row, rows, value):
        hi, lo = split(value)
        for h in range(2):
            merged_hi[h, row : row + rows, :] = hi[:, h * HALF : (h + 1) * HALF]
            merged_lo[h, row : row + rows, :] = lo[:, h * HALF : (h + 1) * HALF]

    norm_slots[x] = jnp.zeros((8, 128), F32)
    norm_slots[x, 0:3, 0:24] = norm_ref[0]

    loads[0].wait()
    loads[1].wait()
    loads[2].wait()
    for m in range(0, 8, 2):
        put(24 * m, 48, jnp.concatenate(
            [ag[0, m].astype(F32) + ae[0, m], ag[0, m + 1].astype(F32) + ae[0, m + 1]], 0))
    loads[3].wait()
    loads[4].wait()
    for m in range(2):
        put(192 + 96 * m, 96, dg[0, m].astype(F32) + de[0, m])

    def project(first, last, row, rows, mask):
        w = split(warm[first:last].reshape((last - first) * RANK, D))
        total = None
        for h in range(2):
            part = dot3(
                [p[:, h * HALF : (h + 1) * HALF] for p in w],
                (merged_hi[h, row : row + rows, :], merged_lo[h, row : row + rows, :]),
                NT,
            )
            total = part if total is None else total + part
        if mask is not None:
            total = fold(jnp.where(mask, total, 0.0), last - first)
        return total

    mask = row_mask(AD_LEFT, AD_ROWS)
    left_a[x] = project(0, 10, 0, AD_ROWS, mask)

    pl.semaphore_wait(barrier, 19)

    def share(buf, i):
        return [
            pltpu.make_async_remote_copy(
                src_ref=buf.at[x], dst_ref=buf.at[x], send_sem=left_send.at[i, d - 1], recv_sem=left_recv.at[i, d - 1],
                device_id=device((x + d) % 4, plane, core), device_id_type=MESH)
            for d in range(1, 4)
        ]

    share_a = share(left_a, 0)
    for copy in share_a:
        copy.start()
    loads[5].wait()
    loads[6].wait()
    for m in range(2):
        put(AD_ROWS + 128 * m, 128, eg[0, 128 * m : 128 * m + 128].astype(F32) + ee[0, 128 * m : 128 * m + 128])
    left_b[x] = project(10, 11, AD_ROWS, 256, None)
    share_b = share(left_b, 1)
    for copy in share_b:
        copy.start()
    share_n = [
        pltpu.make_async_remote_copy(
            src_ref=norm_slots.at[x], dst_ref=norm_slots.at[x], send_sem=norm_send.at[d - 1], recv_sem=norm_recv.at[d - 1],
            device_id=device((x + d) % 4, plane, core), device_id_type=MESH)
        for d in range(1, 4)
    ]
    for copy in share_n:
        copy.start()

    def contract(left, half, row, rows):
        return dot3(left, (merged_hi[half, row : row + rows, :], merged_lo[half, row : row + rows, :]), NN)

    def swap(i, row, rows):
        return pltpu.make_async_remote_copy(
            src_ref=other.at[row : row + rows], dst_ref=sibling.at[row : row + rows], send_sem=core_send.at[i],
            recv_sem=core_recv.at[i], device_id=device(x, plane, 1 - core), device_id_type=MESH)

    for copy in share_a:
        copy.wait_recv()
    pa = (left_a[0] + left_a[1] + left_a[2] + left_a[3]) * 0.25
    left_sum[:, 0:AD_ROWS] = pa
    spread = split(jnp.where(mask, jnp.concatenate([pa] * 10, 0), 0.0))
    other[0:AD_LEFT, :] = contract(spread, 1 - core, 0, AD_ROWS)
    swap_a = swap(0, 0, AD_LEFT)
    swap_a.start()
    own[0:AD_LEFT, :] = contract(spread, core, 0, AD_ROWS)

    for copy in share_b:
        copy.wait_recv()
    pb = (left_b[0] + left_b[1] + left_b[2] + left_b[3]) * 0.25
    left_sum[:, AD_ROWS:ROWS] = pb
    pb = split(pb)
    other[AD_LEFT:LEFT, :] = contract(pb, 1 - core, AD_ROWS, 256)
    swap_b = swap(1, AD_LEFT, RANK)
    swap_b.start()
    own[AD_LEFT:LEFT, :] = contract(pb, core, AD_ROWS, 256)
    left_out = pltpu.make_async_copy(left_sum, left_hbm, out_sem.at[0])
    left_out.start()

    swap_a.wait_recv()
    own[0:AD_LEFT, :] = own[0:AD_LEFT, :] + sibling[0:AD_LEFT, :]

    def scatter(i, carry):
        to_x = (x + 2 + i) % 4
        m = i // 4
        to_plane = (3 * m) % 16

        @pl.when((to_x != x) | (to_plane != plane))
        def _():
            pltpu.make_async_remote_copy(
                src_ref=own.at[pl.ds(pl.multiple_of(RANK * m + 8 * to_x, 8), 8)], dst_ref=slots.at[chip], send_sem=rs_send,
                recv_sem=rs_recv, device_id=device(to_x, to_plane, core), device_id_type=MESH).start()

        return carry

    lax.fori_loop(0, 40, scatter, 0)
    swap_b.wait_recv()
    own[AD_LEFT:LEFT, :] = own[AD_LEFT:LEFT, :] + sibling[AD_LEFT:LEFT, :]
    lax.fori_loop(40, 44, scatter, 0)

    @pl.when(owner)
    def _():
        mine = pl.ds(pl.multiple_of(RANK * here + 8 * x, 8), 8)
        slots[chip] = own[mine, :]
        pltpu.make_async_copy(slots.at[0:63], slots.at[0:63], rs_recv).wait()

        def add(i, total):
            return total + slots[i]

        total = lax.fori_loop(1, 64, add, slots[0])
        right[core, mine, :] = total * 0.25

        def gather(i, carry):
            to = (chip + i) % 64
            pltpu.make_async_remote_copy(
                src_ref=right.at[core, mine], dst_ref=right.at[core, mine], send_sem=ag_send,
                recv_sem=ag_recv, device_id=device(to // 16, to % 16, core), device_id_type=MESH).start()
            return carry

        lax.fori_loop(1, 64, gather, 0)
        pltpu.make_async_copy(own.at[0 : LEFT - 8], own.at[0 : LEFT - 8], ag_recv).wait()

    @pl.when(jnp.logical_not(owner))
    def _():
        pltpu.make_async_copy(own, own, ag_recv).wait()

    forward = pltpu.make_async_remote_copy(
        src_ref=right.at[core], dst_ref=right.at[core], send_sem=half_send, recv_sem=half_recv,
        device_id=device(x, plane, 1 - core), device_id_type=MESH)
    forward.start()
    out_own = pltpu.make_async_copy(right.at[core], right_hbm.at[core], out_sem.at[1])
    out_own.start()
    for copy in share_n:
        copy.wait_recv()
    norm_out[...] = norm_slots[0] + norm_slots[1] + norm_slots[2] + norm_slots[3]
    forward.wait_recv()
    out_other = pltpu.make_async_copy(right.at[1 - core], right_hbm.at[1 - core], out_sem.at[2])
    out_other.start()

    for copy in share_a + share_b + share_n + [swap_a, swap_b, forward]:
        copy.wait_send()

    @pl.when(owner)
    def _():
        pltpu.make_async_copy(own.at[0 : LEFT - 8], own.at[0 : LEFT - 8], rs_send).wait()
        pltpu.make_async_copy(slots.at[0:63], slots.at[0:63], ag_send).wait()

    @pl.when(jnp.logical_not(owner))
    def _():
        pltpu.make_async_copy(own, own, rs_send).wait()

    left_out.wait()
    out_own.wait()
    out_other.wait()


def invert(gram):
    lane = lax.broadcasted_iota(jnp.int32, (8, 128), 1)
    column = lane % RANK
    base = lane - column
    sub = lax.broadcasted_iota(jnp.int32, (8, 128), 0)
    a = [[gram[8 * g : 8 * g + 8, 128 * l : 128 * l + 128] for l in range(3)] for g in range(4)]
    for p in range(RANK):
        gp, sp = p // 8, p % 8
        for l in range(3):
            index = base + p
            pick = [jnp.take_along_axis(a[g][l], index, axis=1) for g in range(gp, 4)]
            pivot = pick[0][sp : sp + 1, :]
            row = jnp.where(column[:1] == p, 1.0, a[gp][l][sp : sp + 1, :]) / pivot
            for g in range(gp, 4):
                f = pick[g - gp]
                keep = jnp.where(column == p, 0.0, a[g][l])
                new = keep - f * row
                a[g][l] = jnp.where(sub > sp, new, a[g][l]) if g == gp else new
    out = []
    for g in range(4):
        parts = []
        for l in range(3):
            i = sub + 8 * g
            pivot = jnp.take_along_axis(a[g][l], base + i, axis=1)
            value = jnp.where(column < i, a[g][l], jnp.where(column == i, 1.0, 0.0))
            parts.append(value / jnp.sqrt(pivot))
        out.append(jnp.concatenate(parts, 1))
    return jnp.concatenate(out, 0)


def finish_kernel(
    ag_hbm, dg_hbm, eg_hbm, ae_hbm, de_hbm, ee_hbm, aw_hbm, dw_hbm, ew_hbm, am_hbm, dm_hbm, em_hbm,
    warm_hbm, right_hbm, left_hbm, norm_total, norm_scale, norm_momentum,
    au_hbm, du_hbm, eu_hbm, ac_hbm, dc_hbm, ec_hbm, ar_hbm, dr_hbm, er_hbm, av_hbm, dv_hbm, ev_hbm,
    next_hbm, norm_updated, norm_velocity,
    ag, dg, eg, ae, de, ee, aw, dw, ew, am, dm, em, warm, right, left,
    au, du, eu, ac, dc, ec, ar, dr, er, av, dv, ev, start, wide, in_sem, out_sem,
):
    pairs = [
        (right_hbm, right), (warm_hbm, warm), (left_hbm, left),
        (ag_hbm, ag), (ae_hbm, ae), (am_hbm, am), (aw_hbm, aw),
        (dg_hbm, dg), (de_hbm, de), (dm_hbm, dm), (dw_hbm, dw),
        (eg_hbm, eg), (ee_hbm, ee), (em_hbm, em), (ew_hbm, ew),
    ]
    loads = [pltpu.make_async_copy(a, b, in_sem.at[i]) for i, (a, b) in enumerate(pairs)]
    for copy in loads:
        copy.start()

    velocity = 0.9 * norm_momentum[...] + norm_total[0:3, 0:24] / 4
    norm_velocity[...] = velocity
    norm_updated[...] = norm_scale[...] - 0.05 * velocity

    wide[LEFT:, :] = jnp.zeros((32, D), F32)
    loads[0].wait()
    loads[1].wait()
    wide[0:LEFT, :] = warm[...].reshape(LEFT, D)
    gram = exact(right[0], wide[:, 0:HALF], NT) + exact(right[1], wide[:, HALF:D], NT)
    mi = lax.broadcasted_iota(jnp.int32, (LEFT, HALF), 0) // RANK
    mj = lax.broadcasted_iota(jnp.int32, (LEFT, HALF), 1) // RANK
    same = mi == mj
    gram = fold(jnp.where(same, gram, 0.0), NMAT)
    i = lax.broadcasted_iota(jnp.int32, (RANK, HALF), 0)
    j = lax.broadcasted_iota(jnp.int32, (RANK, HALF), 1)
    gram = jnp.where(j < LEFT, gram, jnp.where(i == j - LEFT, 1.0, 0.0))
    inverse = invert(gram)
    inverse = jnp.where(same, jnp.concatenate([inverse] * NMAT, 0), 0.0)[:, 0:LEFT]
    for h in range(2):
        start[:, h * HALF : (h + 1) * HALF] = exact(inverse, right[h], NN)
    copies = []

    def send(src, dst):
        copy = pltpu.make_async_copy(src, dst, out_sem.at[len(copies)])
        copy.start()
        copies.append(copy)

    send(start, next_hbm)
    loads[2].wait()
    spread = jnp.where(row_mask(LEFT, ROWS), jnp.concatenate([left[...]] * NMAT, 0), 0.0)
    ortho = exact(inverse, spread, NN)
    oh, ol = split(ortho)
    oh, ol = oh.T, ol.T
    sh, sl = split(start[...])

    def approx(row, rows):
        part = slice(row, row + rows)
        return dot3((oh[part], ol[part]), (sh, sl), NN)

    def write(value, g, e, w, m, u, c, r, v):
        r[...] = g[...].astype(F32) + e[...] - value
        velocity = 0.9 * m[...] + value
        updated = w[...] - 0.05 * velocity
        v[...] = velocity
        u[...] = updated
        c[...] = updated.astype(BF16)

    for k in range(3, 7):
        loads[k].wait()
    value = approx(0, 192)
    for m in range(8):
        write(value[24 * m : 24 * m + 24], ag.at[0, m], ae.at[0, m], aw.at[m], am.at[m],
              au.at[m], ac.at[m], ar.at[0, m], av.at[m])
    for a, b in ((au, au_hbm), (ac, ac_hbm), (ar, ar_hbm), (av, av_hbm)):
        send(a, b)
    for k in range(7, 11):
        loads[k].wait()
    for m in range(2):
        write(approx(192 + 96 * m, 96), dg.at[0, m], de.at[0, m], dw.at[m], dm.at[m],
              du.at[m], dc.at[m], dr.at[0, m], dv.at[m])
    for a, b in ((du, du_hbm), (dc, dc_hbm), (dr, dr_hbm), (dv, dv_hbm)):
        send(a, b)
    for k in range(11, 15):
        loads[k].wait()
    for m in range(2):
        part = pl.ds(128 * m, 128)
        write(approx(AD_ROWS + 128 * m, 128), eg.at[0, part], ee.at[0, part], ew.at[part], em.at[part],
              eu.at[part], ec.at[part], er.at[0, part], ev.at[part])
        for a, b in ((eu, eu_hbm), (ec, ec_hbm), (ev, ev_hbm)):
            send(a.at[part], b.at[part])
        send(er.at[0, part], er_hbm.at[0, part])
    for copy in copies:
        copy.wait()


ANY = pl.BlockSpec(memory_space=pl.ANY)
VMEM = pl.BlockSpec(memory_space=pltpu.VMEM)
DMA = pltpu.SemaphoreType.DMA


def body(
    attention_grad, dense_grad, embedding_grad, attention_error, dense_error, embedding_error,
    attention_weight, dense_weight, embedding_weight, attention_momentum, dense_momentum, embedding_momentum,
    warm_start, norm_scale, norm_momentum, norm_grad,
):
    grads = [attention_grad, dense_grad, embedding_grad]
    errors = [attention_error, dense_error, embedding_error]
    weights = [attention_weight, dense_weight, embedding_weight]
    momenta = [attention_momentum, dense_momentum, embedding_momentum]

    def like(arrays, dtype=None):
        return [pltpu.VMEM(a.shape, dtype or a.dtype) for a in arrays]

    right, left, norm_total = pl.pallas_call(
        exchange_kernel,
        name="exchange",
        out_shape=(
            jax.ShapeDtypeStruct((2, LEFT, HALF), F32),
            jax.ShapeDtypeStruct((RANK, ROWS), F32),
            jax.ShapeDtypeStruct((8, 128), F32),
        ),
        in_specs=[ANY] * 7 + [VMEM],
        out_specs=(ANY, ANY, VMEM),
        scratch_shapes=like(grads) + like(errors) + like([warm_start]) + [
            pltpu.VMEM((2, ROWS, HALF), BF16),
            pltpu.VMEM((2, ROWS, HALF), BF16),
            pltpu.VMEM((4, RANK, AD_ROWS), F32),
            pltpu.VMEM((4, RANK, 256), F32),
            pltpu.VMEM((RANK, ROWS), F32),
            pltpu.VMEM((LEFT, HALF), F32),
            pltpu.VMEM((LEFT, HALF), F32),
            pltpu.VMEM((LEFT, HALF), F32),
            pltpu.VMEM((64, 8, HALF), F32),
            pltpu.VMEM((2, LEFT, HALF), F32),
            pltpu.VMEM((4, 8, 128), F32),
            DMA((7,)), DMA((2, 3)), DMA((2, 3)), DMA((2,)), DMA((2,)), DMA, DMA,
            DMA, DMA, DMA, DMA, DMA((3,)), DMA((3,)), DMA((3,)),
        ],
        compiler_params=pltpu.CompilerParams(collective_id=0, has_side_effects=True, vmem_limit_bytes=40 << 20),
    )(*grads, *errors, warm_start, norm_grad)

    shapes = [
        *[jax.ShapeDtypeStruct(a.shape, F32) for a in weights],
        *[jax.ShapeDtypeStruct(a.shape, BF16) for a in weights],
        *[jax.ShapeDtypeStruct(a.shape, F32) for a in errors],
        *[jax.ShapeDtypeStruct(a.shape, F32) for a in weights],
        jax.ShapeDtypeStruct((LEFT, D), F32),
        jax.ShapeDtypeStruct(norm_scale.shape, F32),
        jax.ShapeDtypeStruct(norm_scale.shape, F32),
    ]
    outs = pl.pallas_call(
        finish_kernel,
        name="finish",
        out_shape=tuple(shapes),
        in_specs=[ANY] * 15 + [VMEM] * 3,
        out_specs=tuple([ANY] * 13 + [VMEM] * 2),
        scratch_shapes=like(grads) + like(errors) + like(weights) + like(momenta) + like([warm_start, right, left])
        + like(weights) + like(weights, BF16) + like(errors) + like(weights) + [
            pltpu.VMEM((LEFT, D), F32), pltpu.VMEM((HALF, D), F32), DMA((15,)), DMA((17,)),
        ],
        compiler_params=pltpu.CompilerParams(vmem_limit_bytes=40 << 20),
    )(*grads, *errors, *weights, *momenta, warm_start, right, left, norm_total, norm_scale, norm_momentum)
    outs = list(outs)
    outs[12] = outs[12].reshape(NMAT, RANK, D)
    return tuple(outs)


def solution(mesh):
    matrices = (P(None, "shard", None), P(None, "shard", None), P("shard", None))
    replicas = (P("rep", None, "shard", None), P("rep", None, "shard", None), P("rep", "shard", None))
    norm = P(None, "shard")
    return jax.shard_map(
        body,
        mesh=mesh,
        in_specs=replicas + replicas + matrices + matrices + (P(), norm, norm, P("rep", None, "shard")),
        out_specs=matrices + matrices + replicas + matrices + (P(), norm, norm),
        check_vma=False,
    )
```

```python
import jax
import jax.numpy as jnp
from jax import lax
from jax.experimental import pallas as pl
from jax.experimental.pallas import tpu as pltpu
from jax.sharding import PartitionSpec as P

MESH = pl.DeviceIdType.MESH
F32, BF16 = jnp.float32, jnp.bfloat16
D = 768
HALF = 384
RANK = 32
NMAT = 11
TILES = 3
LEFT = NMAT * RANK
ROWS = 640
AD_ROWS = 384
AD_LEFT = 10 * RANK
NT = (((1,), (1,)), ((), ()))
NN = (((1,), (0,)), ((), ()))
TN = (((0,), (0,)), ((), ()))


def hops(offset):
    return sum(min(d, 4 - d) for d in offset)


OTHERS = sorted(
    [(a, b, c) for a in range(4) for b in range(4) for c in range(4) if a or b or c],
    key=lambda offset: -hops(offset),
)


def split(x):
    hi = x.astype(BF16)
    return hi, (x - hi.astype(F32)).astype(BF16)


def dot(a, b, dims):
    return lax.dot_general(a, b, dims, preferred_element_type=F32)


def dot3(a, b, dims):
    (ah, al), (bh, bl) = a, b
    return dot(ah, bh, dims) + (dot(al, bh, dims) + dot(ah, bl, dims))


def exact(a, b, dims):
    return dot3(split(a), split(b), dims)


def row_mask(lefts, rows):
    m = lax.broadcasted_iota(jnp.int32, (lefts, rows), 0) // RANK
    r = lax.broadcasted_iota(jnp.int32, (lefts, rows), 1)
    low = jnp.where(m < 8, 24 * m, jnp.where(m < 10, 96 * m - 576, AD_ROWS))
    high = low + jnp.where(m < 8, 24, jnp.where(m < 10, 96, 256))
    return (r >= low) & (r < high)


def fold(x, blocks):
    total = x[:RANK]
    for m in range(1, blocks):
        total = total + x[m * RANK : (m + 1) * RANK]
    return total


def position():
    x, s = lax.axis_index("rep"), lax.axis_index("shard")
    return x, s // 2, s % 2


def device(x, plane, core):
    return (x, plane * 2 + core)


def exchange_kernel(
    ag_hbm, dg_hbm, eg_hbm, ae_hbm, de_hbm, ee_hbm, warm_hbm, norm_hbm, *rest,
):
    state_hbm = rest[:6]
    right_out, left_sum, norm_out, merged, warm = rest[6:11]
    state = rest[11:17]
    exchange_body(
        ag_hbm, dg_hbm, eg_hbm, ae_hbm, de_hbm, ee_hbm, warm_hbm, norm_hbm, state_hbm,
        right_out, left_sum, norm_out, merged, warm, state, *rest[17:],
    )


def exchange_body(
    ag_hbm, dg_hbm, eg_hbm, ae_hbm, de_hbm, ee_hbm, warm_hbm, norm_hbm, state_hbm,
    right, left_sum, norm_out, merged, warm, state,
    ag, dg, eg, ae, de, ee, norm, merged_hi, merged_lo,
    left_a, left_b, other, own, sibling, slots_a, slots_b, norm_slots,
    in_sem, left_send, left_recv, core_send, core_recv, rs_send, rs_recv,
    ag_send, ag_recv, tail_send, tail_recv, half_send, half_recv, norm_send, norm_recv,
):
    x, plane, core = position()
    chip = x * 16 + plane
    idle = chip % 21 == 0
    which = chip - 1 - chip // 21

    def block(q):
        return q % TILES, pl.ds(pl.multiple_of(16 * (q // TILES), 16), 16)

    def tail(r):
        return pl.ds(pl.multiple_of(AD_LEFT + 8 * r, 8), 8)

    xs = [x] + [(x + d) % 4 for d in range(1, 4)]
    zs = [plane // 4] + [(plane // 4 + d) % 4 for d in range(1, 4)]
    ys = [plane % 4] + [(plane % 4 + d) % 4 for d in range(1, 4)]

    barrier = pltpu.get_barrier_semaphore()
    pl.semaphore_signal(barrier, inc=1, device_id=device(x, plane, 1 - core), device_id_type=MESH)
    for d in range(1, 4):
        pl.semaphore_signal(barrier, inc=1, device_id=device((x + d) % 4, plane, core), device_id_type=MESH)

    def greet(i, carry):
        pl.semaphore_signal(barrier, inc=1, device_id=device(x, (plane + i) % 16, core), device_id_type=MESH)
        return carry

    lax.fori_loop(1, 16, greet, 0)

    loads = [
        pltpu.make_async_copy(a, b, in_sem.at[i])
        for i, (a, b) in enumerate(
            [(warm_hbm, warm), (ag_hbm, ag), (ae_hbm, ae), (dg_hbm, dg), (de_hbm, de), (eg_hbm, eg), (ee_hbm, ee), (norm_hbm, norm),
             *zip(state_hbm, state)]
        )
    ]
    for copy in loads[:8]:
        copy.start()

    def put(row, rows, value):
        merged[row : row + rows, :] = value
        hi, lo = split(value)
        for h in range(2):
            merged_hi[h, row : row + rows, :] = hi[:, h * HALF : (h + 1) * HALF]
            merged_lo[h, row : row + rows, :] = lo[:, h * HALF : (h + 1) * HALF]

    loads[0].wait()
    loads[1].wait()
    loads[2].wait()
    for m in range(0, 8, 2):
        put(24 * m, 48, jnp.concatenate(
            [ag[0, m].astype(F32) + ae[0, m], ag[0, m + 1].astype(F32) + ae[0, m + 1]], 0))
    loads[3].wait()
    loads[4].wait()
    for m in range(2):
        put(192 + 96 * m, 96, dg[0, m].astype(F32) + de[0, m])

    def project(first, last, row, rows, mask):
        w = split(warm[first:last].reshape((last - first) * RANK, D))
        total = None
        for h in range(2):
            part = dot3(
                [p[:, h * HALF : (h + 1) * HALF] for p in w],
                (merged_hi[h, row : row + rows, :], merged_lo[h, row : row + rows, :]),
                NT,
            )
            total = part if total is None else total + part
        if mask is not None:
            total = fold(jnp.where(mask, total, 0.0), last - first)
        return total

    mask = row_mask(AD_LEFT, AD_ROWS)
    left_a[x] = project(0, 10, 0, AD_ROWS, mask)

    pl.semaphore_wait(barrier, 19)

    def share(buf, i):
        return [
            pltpu.make_async_remote_copy(
                src_ref=buf.at[x], dst_ref=buf.at[x], send_sem=left_send.at[i, d - 1], recv_sem=left_recv.at[i, d - 1],
                device_id=device((x + d) % 4, plane, core), device_id_type=MESH)
            for d in range(1, 4)
        ]

    share_a = share(left_a, 0)
    for copy in share_a:
        copy.start()
    loads[5].wait()
    loads[6].wait()
    for m in range(2):
        put(AD_ROWS + 128 * m, 128, eg[0, 128 * m : 128 * m + 128].astype(F32) + ee[0, 128 * m : 128 * m + 128])
    left_b[x] = project(10, 11, AD_ROWS, 256, None)
    share_b = share(left_b, 1)
    for copy in share_b:
        copy.start()
    for copy in loads[8:]:
        copy.start()
    loads[7].wait()
    norm_slots[x] = jnp.zeros((8, 128), F32)
    for k in range(3):
        norm_slots[x, k : k + 1, 0:24] = norm[k]
    share_n = [
        pltpu.make_async_remote_copy(
            src_ref=norm_slots.at[x], dst_ref=norm_slots.at[x], send_sem=norm_send.at[d - 1], recv_sem=norm_recv.at[d - 1],
            device_id=device((x + d) % 4, plane, core), device_id_type=MESH)
        for d in range(1, 4)
    ]
    for copy in share_n:
        copy.start()

    def contract(left, half, row, rows):
        return dot3(left, (merged_hi[half, row : row + rows, :], merged_lo[half, row : row + rows, :]), NN)

    def store(ref, row, rows, value):
        for t in range(TILES):
            ref[t, row : row + rows, :] = value[:, 128 * t : 128 * t + 128]

    def swap(i, row, rows):
        return pltpu.make_async_remote_copy(
            src_ref=other.at[:, row : row + rows], dst_ref=sibling.at[:, row : row + rows], send_sem=core_send.at[i],
            recv_sem=core_recv.at[i], device_id=device(x, plane, 1 - core), device_id_type=MESH)

    for copy in share_a:
        copy.wait_recv()
    pa = (left_a[0] + left_a[1] + left_a[2] + left_a[3]) * 0.25
    left_sum[:, 0:AD_ROWS] = pa
    spread = split(jnp.where(mask, jnp.concatenate([pa] * 10, 0), 0.0))
    store(other, 0, AD_LEFT, contract(spread, 1 - core, 0, AD_ROWS))
    swap_a = swap(0, 0, AD_LEFT)
    swap_a.start()
    store(own, 0, AD_LEFT, contract(spread, core, 0, AD_ROWS))

    for copy in share_b:
        copy.wait_recv()
    pb = (left_b[0] + left_b[1] + left_b[2] + left_b[3]) * 0.25
    left_sum[:, AD_ROWS:ROWS] = pb
    pb = split(pb)
    store(other, AD_LEFT, RANK, contract(pb, 1 - core, AD_ROWS, 256))
    swap_b = swap(1, AD_LEFT, RANK)
    swap_b.start()
    store(own, AD_LEFT, RANK, contract(pb, core, AD_ROWS, 256))

    swap_a.wait_recv()
    own[:, 0:AD_LEFT, :] = own[:, 0:AD_LEFT, :] + sibling[:, 0:AD_LEFT, :]
    for dx, dz, dy in OTHERS:
        to = xs[dx] * 16 + zs[dz] * 4 + ys[dy]

        @pl.when(to % 21 != 0)
        def _():
            tile, rows = block(to - 1 - to // 21)
            pltpu.make_async_remote_copy(
                src_ref=own.at[tile, rows], dst_ref=slots_a.at[chip], send_sem=rs_send, recv_sem=rs_recv,
                device_id=device(xs[dx], zs[dz] * 4 + ys[dy], core), device_id_type=MESH).start()

    swap_b.wait_recv()
    own[:, AD_LEFT:LEFT, :] = own[:, AD_LEFT:LEFT, :] + sibling[:, AD_LEFT:LEFT, :]

    def tail_copies(phase, steps, src, dst, target):
        return [
            pltpu.make_async_remote_copy(
                src_ref=src(steps[d]), dst_ref=dst, send_sem=tail_send.at[phase, d - 1], recv_sem=tail_recv.at[phase, d - 1],
                device_id=target(steps[d]), device_id_type=MESH)
            for d in range(1, 4)
        ]

    def start_all(copies):
        for copy in copies:
            copy.start()
        return copies

    def sum_tails(phase, copies):
        for copy in copies:
            copy.wait_recv()
        return (slots_b[phase, 0] + slots_b[phase, 1]) + (slots_b[phase, 2] + slots_b[phase, 3])

    def at_z(z):
        return device(x, z * 4 + ys[0], core)

    slots_b[0, zs[0]] = own[:, tail(zs[0]), :]
    tails_z = start_all(tail_copies(0, zs, lambda z: own.at[:, tail(z)], slots_b.at[0, zs[0]], at_z))
    slots_b[1, x] = sum_tails(0, tails_z)
    part_x = slots_b.at[1, x]
    tails_x = start_all(tail_copies(1, xs, lambda _: part_x, part_x, lambda to: device(to, plane, core)))
    slots_b[2, ys[0]] = sum_tails(1, tails_x)
    part_y = slots_b.at[2, ys[0]]
    tails_y = start_all(tail_copies(2, ys, lambda _: part_y, part_y, lambda y: device(x, zs[0] * 4 + y, core)))

    def spread_out(part):
        for dx, dz, dy in OTHERS:
            pltpu.make_async_remote_copy(
                src_ref=part, dst_ref=part, send_sem=ag_send, recv_sem=ag_recv.at[x],
                device_id=device(xs[dx], zs[dz] * 4 + ys[dy], core), device_id_type=MESH).start()

    def drain(part, sem):
        pltpu.make_async_copy(part, part, sem).wait()

    @pl.when(jnp.logical_not(idle))
    def _():
        tile, rows = block(which)
        slots_a[chip] = own[tile, rows, :]
        drain(slots_a.at[0:63], rs_recv)
        right[core, tile, rows, :] = lax.fori_loop(1, 64, lambda i, t: t + slots_a[i], slots_a[0]) * 0.25
        spread_out(right.at[core, tile, rows])

    right[core, :, tail(zs[0]), :] = sum_tails(2, tails_y) * 0.25
    part_z = right.at[core, :, tail(zs[0])]
    tails_end = start_all(tail_copies(3, zs, lambda _: part_z, part_z, at_z))

    forwards = []

    def forward(rows):
        part = right.at[core, :, rows]
        copy = pltpu.make_async_remote_copy(
            src_ref=part, dst_ref=part, send_sem=half_send.at[len(forwards)], recv_sem=half_recv.at[len(forwards)],
            device_id=device(x, plane, 1 - core), device_id_type=MESH)
        copy.start()
        forwards.append(copy)

    for d in (0, 1, 3, 2):
        from_x = xs[d]
        if d == 0:

            @pl.when(idle)
            def _():
                drain(slots_a.at[0:15], ag_recv.at[x])

            @pl.when(jnp.logical_not(idle))
            def _():
                drain(slots_a.at[0:14], ag_recv.at[x])
        else:
            drain(slots_a.at[0:15], ag_recv.at[from_x])
        forward(pl.ds(pl.multiple_of(80 * from_x, 16), 80))

    for copy in tails_end:
        copy.wait_recv()
    forward(pl.ds(AD_LEFT, RANK))
    for copy in share_n:
        copy.wait_recv()
    norm_out[...] = norm_slots[0] + norm_slots[1] + norm_slots[2] + norm_slots[3]
    for copy in forwards:
        copy.wait_recv()
    for copy in share_a + share_b + share_n + [swap_a, swap_b] + tails_z + tails_x + tails_y + tails_end + forwards:
        copy.wait_send()

    @pl.when(idle)
    def _():
        drain(slots_a.at[0:60], rs_send)

    @pl.when(jnp.logical_not(idle))
    def _():
        drain(slots_a.at[0:59], rs_send)
        drain(slots_a.at[0:63], ag_send)

    for copy in loads[8:]:
        copy.wait()

def invert(gram):
    lane = lax.broadcasted_iota(jnp.int32, (8, 128), 1)
    column = lane % RANK
    base = lane - column
    sub = lax.broadcasted_iota(jnp.int32, (8, 128), 0)
    a = [[gram[8 * g : 8 * g + 8, 128 * l : 128 * l + 128] for l in range(3)] for g in range(4)]
    for p in range(RANK):
        gp, sp = p // 8, p % 8
        for l in range(3):
            index = base + p
            pick = [jnp.take_along_axis(a[g][l], index, axis=1) for g in range(gp, 4)]
            pivot = pick[0][sp : sp + 1, :]
            row = jnp.where(column[:1] == p, 1.0, a[gp][l][sp : sp + 1, :]) / pivot
            for g in range(gp, 4):
                f = pick[g - gp]
                keep = jnp.where(column == p, 0.0, a[g][l])
                new = keep - f * row
                a[g][l] = jnp.where(sub > sp, new, a[g][l]) if g == gp else new
    out = []
    for g in range(4):
        parts = []
        for l in range(3):
            i = sub + 8 * g
            pivot = jnp.take_along_axis(a[g][l], base + i, axis=1)
            value = jnp.where(column < i, a[g][l], jnp.where(column == i, 1.0, 0.0))
            parts.append(value / jnp.sqrt(pivot))
        out.append(jnp.concatenate(parts, 1))
    return jnp.concatenate(out, 0)


def finish_kernel(
    merged, aw, dw, ew, am, dm, em, warm, right, left, norm_total, norm_scale, norm_momentum,
    au_hbm, du_hbm, eu_hbm, ac_hbm, dc_hbm, ec_hbm, ar_hbm, dr_hbm, er_hbm, av_hbm, dv_hbm, ev_hbm,
    next_hbm, norm_updated, norm_velocity,
    au, du, eu, ac, dc, ec, ar, dr, er, av, dv, ev, start, wide, out_sem,
):
    velocity = 0.9 * norm_momentum[...] + norm_total[0:3, 0:24] / 4
    norm_velocity[...] = velocity
    norm_updated[...] = norm_scale[...] - 0.05 * velocity

    wide[LEFT:, :] = jnp.zeros((32, D), F32)
    wide[0:LEFT, :] = warm[...].reshape(LEFT, D)
    factor = jnp.concatenate([right[h, t] for h in range(2) for t in range(TILES)], 1)
    gram = exact(factor, wide[...], NT)
    mi = lax.broadcasted_iota(jnp.int32, (LEFT, HALF), 0) // RANK
    mj = lax.broadcasted_iota(jnp.int32, (LEFT, HALF), 1) // RANK
    same = mi == mj
    gram = fold(jnp.where(same, gram, 0.0), NMAT)
    i = lax.broadcasted_iota(jnp.int32, (RANK, HALF), 0)
    j = lax.broadcasted_iota(jnp.int32, (RANK, HALF), 1)
    gram = jnp.where(j < LEFT, gram, jnp.where(i == j - LEFT, 1.0, 0.0))
    inverse = invert(gram)
    inverse = jnp.where(same, jnp.concatenate([inverse] * NMAT, 0), 0.0)[:, 0:LEFT]
    start[...] = exact(inverse, factor, NN)
    copies = []

    def send(src, dst):
        copy = pltpu.make_async_copy(src, dst, out_sem.at[len(copies)])
        copy.start()
        copies.append(copy)

    send(start, next_hbm)
    spread = jnp.where(row_mask(LEFT, ROWS), jnp.concatenate([left[...]] * NMAT, 0), 0.0)
    ortho = exact(inverse, spread, NN)
    oh, ol = split(ortho)
    oh, ol = oh.T, ol.T
    sh, sl = split(start[...])

    def approx(row, rows):
        part = slice(row, row + rows)
        return dot3((oh[part], ol[part]), (sh, sl), NN)

    def write(value, row, rows, w, m, u, c, r, v):
        r[...] = merged[row : row + rows, :] - value
        velocity = 0.9 * m[...] + value
        updated = w[...] - 0.05 * velocity
        v[...] = velocity
        u[...] = updated
        c[...] = updated.astype(BF16)

    value = approx(0, 192)
    for m in range(8):
        write(value[24 * m : 24 * m + 24], 24 * m, 24, aw.at[m], am.at[m],
              au.at[m], ac.at[m], ar.at[0, m], av.at[m])
    for a, b in ((au, au_hbm), (ac, ac_hbm), (ar, ar_hbm), (av, av_hbm)):
        send(a, b)
    for m in range(2):
        write(approx(192 + 96 * m, 96), 192 + 96 * m, 96, dw.at[m], dm.at[m],
              du.at[m], dc.at[m], dr.at[0, m], dv.at[m])
    for a, b in ((du, du_hbm), (dc, dc_hbm), (dr, dr_hbm), (dv, dv_hbm)):
        send(a, b)
    for m in range(2):
        part = pl.ds(128 * m, 128)
        write(approx(AD_ROWS + 128 * m, 128), AD_ROWS + 128 * m, 128, ew.at[part], em.at[part],
              eu.at[part], ec.at[part], er.at[0, part], ev.at[part])
        for a, b in ((eu, eu_hbm), (ec, ec_hbm), (ev, ev_hbm)):
            send(a.at[part], b.at[part])
        send(er.at[0, part], er_hbm.at[0, part])
    for copy in copies:
        copy.wait()


ANY = pl.BlockSpec(memory_space=pl.ANY)
VMEM = pl.BlockSpec(memory_space=pltpu.VMEM)
DMA = pltpu.SemaphoreType.DMA


def body(
    attention_grad, dense_grad, embedding_grad, attention_error, dense_error, embedding_error,
    attention_weight, dense_weight, embedding_weight, attention_momentum, dense_momentum, embedding_momentum,
    warm_start, norm_scale, norm_momentum, norm_grad,
):
    def pin(*arrays):
        return [pltpu.with_memory_space_constraint(a, pltpu.HBM) for a in arrays]

    grads = pin(attention_grad, dense_grad, embedding_grad)
    errors = pin(attention_error, dense_error, embedding_error)
    weights = pin(attention_weight, dense_weight, embedding_weight)
    momenta = pin(attention_momentum, dense_momentum, embedding_momentum)
    state = weights + momenta

    def like(arrays, dtype=None):
        return [pltpu.VMEM(a.shape, dtype or a.dtype) for a in arrays]

    def shape(a, dtype=None):
        return jax.ShapeDtypeStruct(a.shape, dtype or a.dtype)

    right, left, norm_total, merged, warm, *state = pl.pallas_call(
        exchange_kernel,
        name="exchange",
        out_shape=(
            jax.ShapeDtypeStruct((2, TILES, LEFT, 128), F32),
            jax.ShapeDtypeStruct((RANK, ROWS), F32),
            jax.ShapeDtypeStruct((8, 128), F32),
            jax.ShapeDtypeStruct((ROWS, D), F32),
            shape(warm_start),
            *[shape(a) for a in state],
        ),
        in_specs=[ANY] * 14,
        out_specs=(VMEM,) * 11,
        scratch_shapes=like(grads) + like(errors) + [
            pltpu.VMEM((3, 1, 24), F32),
            pltpu.VMEM((2, ROWS, HALF), BF16),
            pltpu.VMEM((2, ROWS, HALF), BF16),
            pltpu.VMEM((4, RANK, AD_ROWS), F32),
            pltpu.VMEM((4, RANK, 256), F32),
            pltpu.VMEM((TILES, LEFT, 128), F32),
            pltpu.VMEM((TILES, LEFT, 128), F32),
            pltpu.VMEM((TILES, LEFT, 128), F32),
            pltpu.VMEM((64, 16, 128), F32),
            pltpu.VMEM((3, 4, TILES, 8, 128), F32),
            pltpu.VMEM((4, 8, 128), F32),
            DMA((14,)), DMA((2, 3)), DMA((2, 3)), DMA((2,)), DMA((2,)), DMA, DMA,
            DMA, DMA((4,)), DMA((4, 3)), DMA((4, 3)), DMA((5,)), DMA((5,)), DMA((3,)), DMA((3,)),
        ],
        compiler_params=pltpu.CompilerParams(collective_id=0, has_side_effects=True, vmem_limit_bytes=20 << 20),
    )(*grads, *errors, *pin(warm_start, jnp.transpose(norm_grad, (1, 0, 2))), *state)

    shapes = [
        *[jax.ShapeDtypeStruct(a.shape, F32) for a in weights],
        *[jax.ShapeDtypeStruct(a.shape, BF16) for a in weights],
        *[jax.ShapeDtypeStruct(a.shape, F32) for a in errors],
        *[jax.ShapeDtypeStruct(a.shape, F32) for a in weights],
        jax.ShapeDtypeStruct((LEFT, D), F32),
        jax.ShapeDtypeStruct(norm_scale.shape, F32),
        jax.ShapeDtypeStruct(norm_scale.shape, F32),
    ]
    outs = pl.pallas_call(
        finish_kernel,
        name="finish",
        out_shape=tuple(shapes),
        in_specs=[VMEM] * 13,
        out_specs=tuple([ANY] * 13 + [VMEM] * 2),
        scratch_shapes=like(weights) + like(weights, BF16) + like(errors) + like(weights) + [
            pltpu.VMEM((LEFT, D), F32), pltpu.VMEM((HALF, D), F32), DMA((17,)),
        ],
        compiler_params=pltpu.CompilerParams(vmem_limit_bytes=24 << 20),
    )(merged, *state, warm, right, left, norm_total, norm_scale, norm_momentum)
    outs = list(outs)
    outs[12] = outs[12].reshape(NMAT, RANK, D)
    return tuple(outs)


def solution(mesh):
    matrices = (P(None, "shard", None), P(None, "shard", None), P("shard", None))
    replicas = (P("rep", None, "shard", None), P("rep", None, "shard", None), P("rep", "shard", None))
    norm = P(None, "shard")
    return jax.shard_map(
        body,
        mesh=mesh,
        in_specs=replicas + replicas + matrices + matrices + (P(), norm, norm, P("rep", None, "shard")),
        out_specs=matrices + matrices + replicas + matrices + (P(), norm, norm),
        check_vma=False,
    )
```

```python
import jax
import jax.numpy as jnp
from jax import lax
from jax.experimental import pallas as pl
from jax.experimental.pallas import tpu as pltpu
from jax.sharding import PartitionSpec as P

MESH = pl.DeviceIdType.MESH
F32, BF16 = jnp.float32, jnp.bfloat16
D = 768
HALF = 384
RANK = 32
NMAT = 11
TILES = 3
LEFT = NMAT * RANK
ROWS = 640
AD_ROWS = 384
AD_LEFT = 10 * RANK
NT = (((1,), (1,)), ((), ()))
NN = (((1,), (0,)), ((), ()))
TN = (((0,), (0,)), ((), ()))


def hops(offset):
    return sum(min(d, 4 - d) for d in offset)


OTHERS = sorted(
    [(a, b, c) for a in range(4) for b in range(4) for c in range(4) if a or b or c],
    key=lambda offset: -hops(offset),
)


def split(x):
    hi = x.astype(BF16)
    return hi, (x - hi.astype(F32)).astype(BF16)


def dot(a, b, dims):
    return lax.dot_general(a, b, dims, preferred_element_type=F32)


def dot3(a, b, dims):
    (ah, al), (bh, bl) = a, b
    return dot(ah, bh, dims) + (dot(al, bh, dims) + dot(ah, bl, dims))


def exact(a, b, dims):
    return dot3(split(a), split(b), dims)


def row_mask(lefts, rows):
    m = lax.broadcasted_iota(jnp.int32, (lefts, rows), 0) // RANK
    r = lax.broadcasted_iota(jnp.int32, (lefts, rows), 1)
    low = jnp.where(m < 8, 24 * m, jnp.where(m < 10, 96 * m - 576, AD_ROWS))
    high = low + jnp.where(m < 8, 24, jnp.where(m < 10, 96, 256))
    return (r >= low) & (r < high)


def fold(x, blocks):
    total = x[:RANK]
    for m in range(1, blocks):
        total = total + x[m * RANK : (m + 1) * RANK]
    return total


def position():
    x, s = lax.axis_index("rep"), lax.axis_index("shard")
    return x, s // 2, s % 2


def device(x, plane, core):
    return (x, plane * 2 + core)


def exchange_kernel(
    ag_hbm, dg_hbm, eg_hbm, ae_hbm, de_hbm, ee_hbm, warm_hbm, norm_hbm, *rest,
):
    state_hbm = rest[:6]
    right_out, left_sum, norm_out, merged, warm = rest[6:11]
    state = rest[11:17]
    exchange_body(
        ag_hbm, dg_hbm, eg_hbm, ae_hbm, de_hbm, ee_hbm, warm_hbm, norm_hbm, state_hbm,
        right_out, left_sum, norm_out, merged, warm, state, *rest[17:],
    )


def exchange_body(
    ag_hbm, dg_hbm, eg_hbm, ae_hbm, de_hbm, ee_hbm, warm_hbm, norm_hbm, state_hbm,
    right, left_sum, norm_out, merged, warm, state,
    ag, dg, eg, ae, de, ee, norm, merged_hi, merged_lo,
    left_a, left_b, other, own, sibling, slots_a, slots_b, norm_slots,
    in_sem, left_send, left_recv, core_send, core_recv, rs_send, rs_recv,
    ag_send, ag_recv, tail_send, tail_recv, half_send, half_recv, norm_send, norm_recv,
):
    x, plane, core = position()
    chip = x * 16 + plane
    idle = chip % 21 == 0
    which = chip - 1 - chip // 21

    def block(q):
        return q % TILES, pl.ds(pl.multiple_of(16 * (q // TILES), 16), 16)

    def tail(r):
        return pl.ds(pl.multiple_of(AD_LEFT + 8 * r, 8), 8)

    xs = [x] + [(x + d) % 4 for d in range(1, 4)]
    zs = [plane // 4] + [(plane // 4 + d) % 4 for d in range(1, 4)]
    ys = [plane % 4] + [(plane % 4 + d) % 4 for d in range(1, 4)]

    barrier = pltpu.get_barrier_semaphore()
    pl.semaphore_signal(barrier, inc=1, device_id=device(x, plane, 1 - core), device_id_type=MESH)
    for d in range(1, 4):
        pl.semaphore_signal(barrier, inc=1, device_id=device((x + d) % 4, plane, core), device_id_type=MESH)

    def greet(i, carry):
        pl.semaphore_signal(barrier, inc=1, device_id=device(x, (plane + i) % 16, core), device_id_type=MESH)
        return carry

    lax.fori_loop(1, 16, greet, 0)

    loads = [
        pltpu.make_async_copy(a, b, in_sem.at[i])
        for i, (a, b) in enumerate(
            [(warm_hbm, warm), (ag_hbm, ag), (ae_hbm, ae), (dg_hbm, dg), (de_hbm, de), (eg_hbm, eg), (ee_hbm, ee), (norm_hbm, norm),
             *zip(state_hbm, state)]
        )
    ]
    for copy in loads[:8]:
        copy.start()

    def put(row, rows, value):
        merged[row : row + rows, :] = value
        hi, lo = split(value)
        for h in range(2):
            merged_hi[h, row : row + rows, :] = hi[:, h * HALF : (h + 1) * HALF]
            merged_lo[h, row : row + rows, :] = lo[:, h * HALF : (h + 1) * HALF]

    loads[0].wait()
    loads[1].wait()
    loads[2].wait()
    for m in range(0, 8, 2):
        put(24 * m, 48, jnp.concatenate(
            [ag[0, m].astype(F32) + ae[0, m], ag[0, m + 1].astype(F32) + ae[0, m + 1]], 0))
    loads[3].wait()
    loads[4].wait()
    for m in range(2):
        put(192 + 96 * m, 96, dg[0, m].astype(F32) + de[0, m])

    def project(first, last, row, rows, mask):
        w = split(warm[first:last].reshape((last - first) * RANK, D))
        total = None
        for h in range(2):
            part = dot3(
                [p[:, h * HALF : (h + 1) * HALF] for p in w],
                (merged_hi[h, row : row + rows, :], merged_lo[h, row : row + rows, :]),
                NT,
            )
            total = part if total is None else total + part
        if mask is not None:
            total = fold(jnp.where(mask, total, 0.0), last - first)
        return total

    mask = row_mask(AD_LEFT, AD_ROWS)
    left_a[x] = project(0, 10, 0, AD_ROWS, mask)

    pl.semaphore_wait(barrier, 19)

    def share(buf, i):
        return [
            pltpu.make_async_remote_copy(
                src_ref=buf.at[x], dst_ref=buf.at[x], send_sem=left_send.at[i, d - 1], recv_sem=left_recv.at[i, d - 1],
                device_id=device((x + d) % 4, plane, core), device_id_type=MESH)
            for d in range(1, 4)
        ]

    share_a = share(left_a, 0)
    for copy in share_a:
        copy.start()
    loads[5].wait()
    loads[6].wait()
    for m in range(2):
        put(AD_ROWS + 128 * m, 128, eg[0, 128 * m : 128 * m + 128].astype(F32) + ee[0, 128 * m : 128 * m + 128])
    left_b[x] = project(10, 11, AD_ROWS, 256, None)
    share_b = share(left_b, 1)
    for copy in share_b:
        copy.start()
    for copy in loads[8:]:
        copy.start()
    loads[7].wait()
    norm_slots[x] = jnp.zeros((8, 128), F32)
    for k in range(3):
        norm_slots[x, k : k + 1, 0:24] = norm[k]
    share_n = [
        pltpu.make_async_remote_copy(
            src_ref=norm_slots.at[x], dst_ref=norm_slots.at[x], send_sem=norm_send.at[d - 1], recv_sem=norm_recv.at[d - 1],
            device_id=device((x + d) % 4, plane, core), device_id_type=MESH)
        for d in range(1, 4)
    ]
    for copy in share_n:
        copy.start()

    def contract(left, half, row, rows):
        return dot3(left, (merged_hi[half, row : row + rows, :], merged_lo[half, row : row + rows, :]), NN)

    def store(ref, row, rows, value):
        for t in range(TILES):
            ref[t, row : row + rows, :] = value[:, 128 * t : 128 * t + 128]

    def swap(i, row, rows):
        return pltpu.make_async_remote_copy(
            src_ref=other.at[:, row : row + rows], dst_ref=sibling.at[:, row : row + rows], send_sem=core_send.at[i],
            recv_sem=core_recv.at[i], device_id=device(x, plane, 1 - core), device_id_type=MESH)

    for copy in share_a:
        copy.wait_recv()
    pa = (left_a[0] + left_a[1] + left_a[2] + left_a[3]) * 0.25
    left_sum[:, 0:AD_ROWS] = pa
    spread = split(jnp.where(mask, jnp.concatenate([pa] * 10, 0), 0.0))
    store(other, 0, AD_LEFT, contract(spread, 1 - core, 0, AD_ROWS))
    swap_a = swap(0, 0, AD_LEFT)
    swap_a.start()
    store(own, 0, AD_LEFT, contract(spread, core, 0, AD_ROWS))

    for copy in share_b:
        copy.wait_recv()
    pb = (left_b[0] + left_b[1] + left_b[2] + left_b[3]) * 0.25
    left_sum[:, AD_ROWS:ROWS] = pb
    pb = split(pb)
    store(other, AD_LEFT, RANK, contract(pb, 1 - core, AD_ROWS, 256))
    swap_b = swap(1, AD_LEFT, RANK)
    swap_b.start()
    store(own, AD_LEFT, RANK, contract(pb, core, AD_ROWS, 256))

    swap_a.wait_recv()
    own[:, 0:AD_LEFT, :] = own[:, 0:AD_LEFT, :] + sibling[:, 0:AD_LEFT, :]
    def scatter(others):
        for dx, dz, dy in others:
            to = xs[dx] * 16 + zs[dz] * 4 + ys[dy]

            @pl.when(to % 21 != 0)
            def _():
                tile, rows = block(to - 1 - to // 21)
                pltpu.make_async_remote_copy(
                    src_ref=own.at[tile, rows], dst_ref=slots_a.at[chip], send_sem=rs_send, recv_sem=rs_recv,
                    device_id=device(xs[dx], zs[dz] * 4 + ys[dy], core), device_id_type=MESH).start()

    swap_b.wait_recv()
    own[:, AD_LEFT:LEFT, :] = own[:, AD_LEFT:LEFT, :] + sibling[:, AD_LEFT:LEFT, :]

    def tail_copies(phase, steps, src, dst, target):
        return [
            pltpu.make_async_remote_copy(
                src_ref=src(steps[d]), dst_ref=dst, send_sem=tail_send.at[phase, d - 1], recv_sem=tail_recv.at[phase, d - 1],
                device_id=target(steps[d]), device_id_type=MESH)
            for d in range(1, 4)
        ]

    def start_all(copies):
        for copy in copies:
            copy.start()
        return copies

    def sum_tails(phase, copies):
        for copy in copies:
            copy.wait_recv()
        return (slots_b[phase, 0] + slots_b[phase, 1]) + (slots_b[phase, 2] + slots_b[phase, 3])

    def at_z(z):
        return device(x, z * 4 + ys[0], core)

    slots_b[0, zs[0]] = own[:, tail(zs[0]), :]
    tails_z = start_all(tail_copies(0, zs, lambda z: own.at[:, tail(z)], slots_b.at[0, zs[0]], at_z))
    scatter(OTHERS)
    slots_b[1, x] = sum_tails(0, tails_z)
    part_x = slots_b.at[1, x]
    tails_x = start_all(tail_copies(1, xs, lambda _: part_x, part_x, lambda to: device(to, plane, core)))
    slots_b[2, ys[0]] = sum_tails(1, tails_x)
    part_y = slots_b.at[2, ys[0]]
    tails_y = start_all(tail_copies(2, ys, lambda _: part_y, part_y, lambda y: device(x, zs[0] * 4 + y, core)))

    def spread_out(part):
        for dx, dz, dy in OTHERS:
            pltpu.make_async_remote_copy(
                src_ref=part, dst_ref=part, send_sem=ag_send, recv_sem=ag_recv.at[x],
                device_id=device(xs[dx], zs[dz] * 4 + ys[dy], core), device_id_type=MESH).start()

    def drain(part, sem):
        pltpu.make_async_copy(part, part, sem).wait()

    @pl.when(jnp.logical_not(idle))
    def _():
        tile, rows = block(which)
        slots_a[chip] = own[tile, rows, :]
        drain(slots_a.at[0:63], rs_recv)
        right[core, tile, rows, :] = jnp.sum(slots_a[...], axis=0) * 0.25
        spread_out(right.at[core, tile, rows])

    right[core, :, tail(zs[0]), :] = sum_tails(2, tails_y) * 0.25
    part_z = right.at[core, :, tail(zs[0])]
    tails_end = start_all(tail_copies(3, zs, lambda _: part_z, part_z, at_z))

    forwards = []

    def forward(rows):
        part = right.at[core, :, rows]
        copy = pltpu.make_async_remote_copy(
            src_ref=part, dst_ref=part, send_sem=half_send.at[len(forwards)], recv_sem=half_recv.at[len(forwards)],
            device_id=device(x, plane, 1 - core), device_id_type=MESH)
        copy.start()
        forwards.append(copy)

    for d in (0, 1, 3, 2):
        from_x = xs[d]
        if d == 0:

            @pl.when(idle)
            def _():
                drain(slots_a.at[0:15], ag_recv.at[x])

            @pl.when(jnp.logical_not(idle))
            def _():
                drain(slots_a.at[0:14], ag_recv.at[x])
        else:
            drain(slots_a.at[0:15], ag_recv.at[from_x])
        forward(pl.ds(pl.multiple_of(80 * from_x, 16), 80))

    for copy in tails_end:
        copy.wait_recv()
    forward(pl.ds(AD_LEFT, RANK))
    for copy in share_n:
        copy.wait_recv()
    norm_out[...] = norm_slots[0] + norm_slots[1] + norm_slots[2] + norm_slots[3]
    for copy in forwards:
        copy.wait_recv()
    for copy in share_a + share_b + share_n + [swap_a, swap_b] + tails_z + tails_x + tails_y + tails_end + forwards:
        copy.wait_send()

    @pl.when(idle)
    def _():
        drain(slots_a.at[0:60], rs_send)

    @pl.when(jnp.logical_not(idle))
    def _():
        drain(slots_a.at[0:59], rs_send)
        drain(slots_a.at[0:63], ag_send)

    for copy in loads[8:]:
        copy.wait()

def invert(gram):
    lane = lax.broadcasted_iota(jnp.int32, (8, 128), 1)
    column = lane % RANK
    base = lane - column
    sub = lax.broadcasted_iota(jnp.int32, (8, 128), 0)
    a = [[gram[8 * g : 8 * g + 8, 128 * l : 128 * l + 128] for l in range(3)] for g in range(4)]
    picks = [[jnp.take_along_axis(a[g][l], base, axis=1) for g in range(4)] for l in range(3)]
    for p in range(RANK):
        gp, sp = p // 8, p % 8
        for l in range(3):
            pick = picks[l]
            pivot = pick[0][sp : sp + 1, :]
            if p + 1 < RANK:
                ahead = [jnp.take_along_axis(a[g][l], base + p + 1, axis=1) for g in range(gp, 4)]
                ratio = ahead[0][sp : sp + 1, :] / pivot
                ahead = [c - f * ratio for c, f in zip(ahead, pick)]
                picks[l] = ahead[(p + 1) // 8 - gp :]
            row = jnp.where(column[:1] == p, 1.0, a[gp][l][sp : sp + 1, :]) / pivot
            for g in range(gp, 4):
                f = pick[g - gp]
                keep = jnp.where(column == p, 0.0, a[g][l])
                new = keep - f * row
                a[g][l] = jnp.where(sub > sp, new, a[g][l]) if g == gp else new
    out = []
    for g in range(4):
        parts = []
        for l in range(3):
            i = sub + 8 * g
            pivot = jnp.take_along_axis(a[g][l], base + i, axis=1)
            value = jnp.where(column < i, a[g][l], jnp.where(column == i, 1.0, 0.0))
            parts.append(value / jnp.sqrt(pivot))
        out.append(jnp.concatenate(parts, 1))
    return jnp.concatenate(out, 0)


def finish_kernel(
    merged, aw, dw, ew, am, dm, em, warm, right, left, norm_total, norm_scale, norm_momentum,
    au_hbm, du_hbm, eu_hbm, ac_hbm, dc_hbm, ec_hbm, ar_hbm, dr_hbm, er_hbm, av_hbm, dv_hbm, ev_hbm,
    next_hbm, norm_updated, norm_velocity,
    au, du, eu, ac, dc, ec, ar, dr, er, av, dv, ev, start, wide, out_sem,
):
    velocity = 0.9 * norm_momentum[...] + norm_total[0:3, 0:24] / 4
    norm_velocity[...] = velocity
    norm_updated[...] = norm_scale[...] - 0.05 * velocity

    wide[LEFT:, :] = jnp.zeros((32, D), F32)
    wide[0:LEFT, :] = warm[...].reshape(LEFT, D)
    factor = jnp.concatenate([right[h, t] for h in range(2) for t in range(TILES)], 1)
    gram = exact(factor, wide[...], NT)
    mi = lax.broadcasted_iota(jnp.int32, (LEFT, HALF), 0) // RANK
    mj = lax.broadcasted_iota(jnp.int32, (LEFT, HALF), 1) // RANK
    same = mi == mj
    gram = fold(jnp.where(same, gram, 0.0), NMAT)
    i = lax.broadcasted_iota(jnp.int32, (RANK, HALF), 0)
    j = lax.broadcasted_iota(jnp.int32, (RANK, HALF), 1)
    gram = jnp.where(j < LEFT, gram, jnp.where(i == j - LEFT, 1.0, 0.0))
    inverse = invert(gram)
    inverse = jnp.where(same, jnp.concatenate([inverse] * NMAT, 0), 0.0)[:, 0:LEFT]
    start[...] = exact(inverse, factor, NN)
    copies = []

    def send(src, dst):
        copy = pltpu.make_async_copy(src, dst, out_sem.at[len(copies)])
        copy.start()
        copies.append(copy)

    send(start, next_hbm)
    spread = jnp.where(row_mask(LEFT, ROWS), jnp.concatenate([left[...]] * NMAT, 0), 0.0)
    ortho = exact(inverse, spread, NN)
    oh, ol = split(ortho)
    oh, ol = oh.T, ol.T
    sh, sl = split(start[...])

    def approx(row, rows):
        part = slice(row, row + rows)
        return dot3((oh[part], ol[part]), (sh, sl), NN)

    def write(value, row, rows, w, m, u, c, r, v):
        r[...] = merged[row : row + rows, :] - value
        velocity = 0.9 * m[...] + value
        updated = w[...] - 0.05 * velocity
        v[...] = velocity
        u[...] = updated
        c[...] = updated.astype(BF16)

    value = approx(0, 192)
    for m in range(8):
        write(value[24 * m : 24 * m + 24], 24 * m, 24, aw.at[m], am.at[m],
              au.at[m], ac.at[m], ar.at[0, m], av.at[m])
    for a, b in ((au, au_hbm), (ac, ac_hbm), (ar, ar_hbm), (av, av_hbm)):
        send(a, b)
    for m in range(2):
        write(approx(192 + 96 * m, 96), 192 + 96 * m, 96, dw.at[m], dm.at[m],
              du.at[m], dc.at[m], dr.at[0, m], dv.at[m])
    for a, b in ((du, du_hbm), (dc, dc_hbm), (dr, dr_hbm), (dv, dv_hbm)):
        send(a, b)
    for m in range(2):
        part = pl.ds(128 * m, 128)
        write(approx(AD_ROWS + 128 * m, 128), AD_ROWS + 128 * m, 128, ew.at[part], em.at[part],
              eu.at[part], ec.at[part], er.at[0, part], ev.at[part])
        for a, b in ((eu, eu_hbm), (ec, ec_hbm), (ev, ev_hbm)):
            send(a.at[part], b.at[part])
        send(er.at[0, part], er_hbm.at[0, part])
    for copy in copies:
        copy.wait()


ANY = pl.BlockSpec(memory_space=pl.ANY)
VMEM = pl.BlockSpec(memory_space=pltpu.VMEM)
DMA = pltpu.SemaphoreType.DMA


def body(
    attention_grad, dense_grad, embedding_grad, attention_error, dense_error, embedding_error,
    attention_weight, dense_weight, embedding_weight, attention_momentum, dense_momentum, embedding_momentum,
    warm_start, norm_scale, norm_momentum, norm_grad,
):
    def pin(*arrays):
        return [pltpu.with_memory_space_constraint(a, pltpu.HBM) for a in arrays]

    grads = pin(attention_grad, dense_grad, embedding_grad)
    errors = pin(attention_error, dense_error, embedding_error)
    weights = pin(attention_weight, dense_weight, embedding_weight)
    momenta = pin(attention_momentum, dense_momentum, embedding_momentum)
    state = weights + momenta

    def like(arrays, dtype=None):
        return [pltpu.VMEM(a.shape, dtype or a.dtype) for a in arrays]

    def shape(a, dtype=None):
        return jax.ShapeDtypeStruct(a.shape, dtype or a.dtype)

    right, left, norm_total, merged, warm, *state = pl.pallas_call(
        exchange_kernel,
        name="exchange",
        out_shape=(
            jax.ShapeDtypeStruct((2, TILES, LEFT, 128), F32),
            jax.ShapeDtypeStruct((RANK, ROWS), F32),
            jax.ShapeDtypeStruct((8, 128), F32),
            jax.ShapeDtypeStruct((ROWS, D), F32),
            shape(warm_start),
            *[shape(a) for a in state],
        ),
        in_specs=[ANY] * 14,
        out_specs=(VMEM,) * 11,
        scratch_shapes=like(grads) + like(errors) + [
            pltpu.VMEM((3, 1, 24), F32),
            pltpu.VMEM((2, ROWS, HALF), BF16),
            pltpu.VMEM((2, ROWS, HALF), BF16),
            pltpu.VMEM((4, RANK, AD_ROWS), F32),
            pltpu.VMEM((4, RANK, 256), F32),
            pltpu.VMEM((TILES, LEFT, 128), F32),
            pltpu.VMEM((TILES, LEFT, 128), F32),
            pltpu.VMEM((TILES, LEFT, 128), F32),
            pltpu.VMEM((64, 16, 128), F32),
            pltpu.VMEM((3, 4, TILES, 8, 128), F32),
            pltpu.VMEM((4, 8, 128), F32),
            DMA((14,)), DMA((2, 3)), DMA((2, 3)), DMA((2,)), DMA((2,)), DMA, DMA,
            DMA, DMA((4,)), DMA((4, 3)), DMA((4, 3)), DMA((5,)), DMA((5,)), DMA((3,)), DMA((3,)),
        ],
        compiler_params=pltpu.CompilerParams(collective_id=0, has_side_effects=True, vmem_limit_bytes=20 << 20),
    )(*grads, *errors, *pin(warm_start, jnp.transpose(norm_grad, (1, 0, 2))), *state)

    shapes = [
        *[jax.ShapeDtypeStruct(a.shape, F32) for a in weights],
        *[jax.ShapeDtypeStruct(a.shape, BF16) for a in weights],
        *[jax.ShapeDtypeStruct(a.shape, F32) for a in errors],
        *[jax.ShapeDtypeStruct(a.shape, F32) for a in weights],
        jax.ShapeDtypeStruct((LEFT, D), F32),
        jax.ShapeDtypeStruct(norm_scale.shape, F32),
        jax.ShapeDtypeStruct(norm_scale.shape, F32),
    ]
    outs = pl.pallas_call(
        finish_kernel,
        name="finish",
        out_shape=tuple(shapes),
        in_specs=[VMEM] * 13,
        out_specs=tuple([ANY] * 13 + [VMEM] * 2),
        scratch_shapes=like(weights) + like(weights, BF16) + like(errors) + like(weights) + [
            pltpu.VMEM((LEFT, D), F32), pltpu.VMEM((HALF, D), F32), DMA((17,)),
        ],
        compiler_params=pltpu.CompilerParams(vmem_limit_bytes=24 << 20),
    )(merged, *state, warm, right, left, norm_total, norm_scale, norm_momentum)
    outs = list(outs)
    outs[12] = outs[12].reshape(NMAT, RANK, D)
    return tuple(outs)


def solution(mesh):
    matrices = (P(None, "shard", None), P(None, "shard", None), P("shard", None))
    replicas = (P("rep", None, "shard", None), P("rep", None, "shard", None), P("rep", "shard", None))
    norm = P(None, "shard")
    return jax.shard_map(
        body,
        mesh=mesh,
        in_specs=replicas + replicas + matrices + matrices + (P(), norm, norm, P("rep", None, "shard")),
        out_specs=matrices + matrices + replicas + matrices + (P(), norm, norm),
        check_vma=False,
    )
```

```python
import jax
import jax.numpy as jnp
from jax import lax
from jax.experimental import pallas as pl
from jax.experimental.pallas import tpu as pltpu
from jax.sharding import PartitionSpec as P

MESH = pl.DeviceIdType.MESH
F32, BF16 = jnp.float32, jnp.bfloat16
D = 768
HALF = 384
RANK = 32
NMAT = 11
TILES = 3
LEFT = NMAT * RANK
ROWS = 640
AD_ROWS = 384
AD_LEFT = 10 * RANK
NT = (((1,), (1,)), ((), ()))
NN = (((1,), (0,)), ((), ()))
TN = (((0,), (0,)), ((), ()))


def hops(offset):
    return sum(min(d, 4 - d) for d in offset)


OTHERS = sorted(
    [(a, b, c) for a in range(4) for b in range(4) for c in range(4) if a or b or c],
    key=lambda offset: -hops(offset),
)


def split(x):
    hi = x.astype(BF16)
    return hi, (x - hi.astype(F32)).astype(BF16)


def dot(a, b, dims):
    return lax.dot_general(a, b, dims, preferred_element_type=F32)


def dot3(a, b, dims):
    (ah, al), (bh, bl) = a, b
    return dot(ah, bh, dims) + (dot(al, bh, dims) + dot(ah, bl, dims))


def exact(a, b, dims):
    return dot3(split(a), split(b), dims)


def row_mask(lefts, rows):
    m = lax.broadcasted_iota(jnp.int32, (lefts, rows), 0) // RANK
    r = lax.broadcasted_iota(jnp.int32, (lefts, rows), 1)
    low = jnp.where(m < 8, 24 * m, jnp.where(m < 10, 96 * m - 576, AD_ROWS))
    high = low + jnp.where(m < 8, 24, jnp.where(m < 10, 96, 256))
    return (r >= low) & (r < high)


def fold(x, blocks):
    total = x[:RANK]
    for m in range(1, blocks):
        total = total + x[m * RANK : (m + 1) * RANK]
    return total


def position():
    x, s = lax.axis_index("rep"), lax.axis_index("shard")
    return x, s // 2, s % 2


def device(x, plane, core):
    return (x, plane * 2 + core)


def exchange_kernel(
    ag_hbm, dg_hbm, eg_hbm, ae_hbm, de_hbm, ee_hbm, warm_hbm, norm_hbm, *rest,
):
    state_hbm = rest[:6]
    right_out, left_sum, norm_out, merged, warm = rest[6:11]
    state = rest[11:17]
    exchange_body(
        ag_hbm, dg_hbm, eg_hbm, ae_hbm, de_hbm, ee_hbm, warm_hbm, norm_hbm, state_hbm,
        right_out, left_sum, norm_out, merged, warm, state, *rest[17:],
    )


def exchange_body(
    ag_hbm, dg_hbm, eg_hbm, ae_hbm, de_hbm, ee_hbm, warm_hbm, norm_hbm, state_hbm,
    right, left_sum, norm_out, merged, warm, state,
    ag, dg, eg, ae, de, ee, norm, merged_hi, merged_lo,
    left_a, left_b, other, own, sibling, slots_a, slots_b, norm_slots,
    in_sem, left_send, left_recv, core_send, core_recv, rs_send, rs_recv,
    ag_send, ag_recv, tail_send, tail_recv, half_send, half_recv, norm_send, norm_recv,
):
    x, plane, core = position()
    chip = x * 16 + plane
    idle = chip % 21 == 0
    which = chip - 1 - chip // 21

    def block(q):
        return q % TILES, pl.ds(pl.multiple_of(16 * (q // TILES), 16), 16)

    def tail(r):
        return pl.ds(pl.multiple_of(AD_LEFT + 8 * r, 8), 8)

    xs = [x] + [(x + d) % 4 for d in range(1, 4)]
    zs = [plane // 4] + [(plane // 4 + d) % 4 for d in range(1, 4)]
    ys = [plane % 4] + [(plane % 4 + d) % 4 for d in range(1, 4)]

    barrier = pltpu.get_barrier_semaphore()
    pl.semaphore_signal(barrier, inc=1, device_id=device(x, plane, 1 - core), device_id_type=MESH)
    for d in range(1, 4):
        pl.semaphore_signal(barrier, inc=1, device_id=device((x + d) % 4, plane, core), device_id_type=MESH)

    def greet(i, carry):
        pl.semaphore_signal(barrier, inc=1, device_id=device(x, (plane + i) % 16, core), device_id_type=MESH)
        return carry

    lax.fori_loop(1, 16, greet, 0)

    loads = [
        pltpu.make_async_copy(a, b, in_sem.at[i])
        for i, (a, b) in enumerate(
            [(warm_hbm, warm), (ag_hbm, ag), (ae_hbm, ae), (dg_hbm, dg), (de_hbm, de), (eg_hbm, eg), (ee_hbm, ee), (norm_hbm, norm),
             *zip(state_hbm, state)]
        )
    ]
    for copy in loads[:8]:
        copy.start()

    def put(row, rows, value):
        merged[row : row + rows, :] = value
        hi, lo = split(value)
        for h in range(2):
            merged_hi[h, row : row + rows, :] = hi[:, h * HALF : (h + 1) * HALF]
            merged_lo[h, row : row + rows, :] = lo[:, h * HALF : (h + 1) * HALF]

    loads[0].wait()
    loads[1].wait()
    loads[2].wait()
    for m in range(0, 8, 2):
        put(24 * m, 48, jnp.concatenate(
            [ag[0, m].astype(F32) + ae[0, m], ag[0, m + 1].astype(F32) + ae[0, m + 1]], 0))
    loads[3].wait()
    loads[4].wait()
    for m in range(2):
        put(192 + 96 * m, 96, dg[0, m].astype(F32) + de[0, m])

    def project(first, last, row, rows, mask):
        w = split(warm[first:last].reshape((last - first) * RANK, D))
        total = None
        for h in range(2):
            part = dot3(
                [p[:, h * HALF : (h + 1) * HALF] for p in w],
                (merged_hi[h, row : row + rows, :], merged_lo[h, row : row + rows, :]),
                NT,
            )
            total = part if total is None else total + part
        if mask is not None:
            total = fold(jnp.where(mask, total, 0.0), last - first)
        return total

    mask = row_mask(AD_LEFT, AD_ROWS)
    left_a[x] = project(0, 10, 0, AD_ROWS, mask)

    pl.semaphore_wait(barrier, 19)

    def share(buf, i):
        return [
            pltpu.make_async_remote_copy(
                src_ref=buf.at[x], dst_ref=buf.at[x], send_sem=left_send.at[i, d - 1], recv_sem=left_recv.at[i, d - 1],
                device_id=device((x + d) % 4, plane, core), device_id_type=MESH)
            for d in range(1, 4)
        ]

    share_a = share(left_a, 0)
    for copy in share_a:
        copy.start()
    loads[5].wait()
    loads[6].wait()
    for m in range(2):
        put(AD_ROWS + 128 * m, 128, eg[0, 128 * m : 128 * m + 128].astype(F32) + ee[0, 128 * m : 128 * m + 128])
    left_b[x] = project(10, 11, AD_ROWS, 256, None)
    share_b = share(left_b, 1)
    for copy in share_b:
        copy.start()
    for copy in loads[8:]:
        copy.start()
    loads[7].wait()
    norm_slots[x] = jnp.zeros((8, 128), F32)
    for k in range(3):
        norm_slots[x, k : k + 1, 0:24] = norm[k]
    share_n = [
        pltpu.make_async_remote_copy(
            src_ref=norm_slots.at[x], dst_ref=norm_slots.at[x], send_sem=norm_send.at[d - 1], recv_sem=norm_recv.at[d - 1],
            device_id=device((x + d) % 4, plane, core), device_id_type=MESH)
        for d in range(1, 4)
    ]
    for copy in share_n:
        copy.start()

    def contract(left, half, row, rows):
        return dot3(left, (merged_hi[half, row : row + rows, :], merged_lo[half, row : row + rows, :]), NN)

    def store(ref, row, rows, value):
        for t in range(TILES):
            ref[t, row : row + rows, :] = value[:, 128 * t : 128 * t + 128]

    def swap(i, row, rows):
        return pltpu.make_async_remote_copy(
            src_ref=other.at[:, row : row + rows], dst_ref=sibling.at[:, row : row + rows], send_sem=core_send.at[i],
            recv_sem=core_recv.at[i], device_id=device(x, plane, 1 - core), device_id_type=MESH)

    for copy in share_a:
        copy.wait_recv()
    pa = (left_a[0] + left_a[1] + left_a[2] + left_a[3]) * 0.25
    left_sum[:, 0:AD_ROWS] = pa
    spread = split(jnp.where(mask, jnp.concatenate([pa] * 10, 0), 0.0))
    store(other, 0, AD_LEFT, contract(spread, 1 - core, 0, AD_ROWS))
    swap_a = swap(0, 0, AD_LEFT)
    swap_a.start()
    store(own, 0, AD_LEFT, contract(spread, core, 0, AD_ROWS))

    for copy in share_b:
        copy.wait_recv()
    pb = (left_b[0] + left_b[1] + left_b[2] + left_b[3]) * 0.25
    left_sum[:, AD_ROWS:ROWS] = pb
    pb = split(pb)
    store(other, AD_LEFT, RANK, contract(pb, 1 - core, AD_ROWS, 256))
    swap_b = swap(1, AD_LEFT, RANK)
    swap_b.start()
    store(own, AD_LEFT, RANK, contract(pb, core, AD_ROWS, 256))

    swap_a.wait_recv()
    own[:, 0:AD_LEFT, :] = own[:, 0:AD_LEFT, :] + sibling[:, 0:AD_LEFT, :]
    def scatter(others):
        for dx, dz, dy in others:
            to = xs[dx] * 16 + zs[dz] * 4 + ys[dy]

            @pl.when(to % 21 != 0)
            def _():
                tile, rows = block(to - 1 - to // 21)
                pltpu.make_async_remote_copy(
                    src_ref=own.at[tile, rows], dst_ref=slots_a.at[chip], send_sem=rs_send, recv_sem=rs_recv,
                    device_id=device(xs[dx], zs[dz] * 4 + ys[dy], core), device_id_type=MESH).start()

    swap_b.wait_recv()
    own[:, AD_LEFT:LEFT, :] = own[:, AD_LEFT:LEFT, :] + sibling[:, AD_LEFT:LEFT, :]

    def tail_copies(phase, steps, src, dst, target):
        return [
            pltpu.make_async_remote_copy(
                src_ref=src(steps[d]), dst_ref=dst, send_sem=tail_send.at[phase, d - 1], recv_sem=tail_recv.at[phase, d - 1],
                device_id=target(steps[d]), device_id_type=MESH)
            for d in range(1, 4)
        ]

    def start_all(copies):
        for copy in copies:
            copy.start()
        return copies

    def sum_tails(phase, copies):
        for copy in copies:
            copy.wait_recv()
        return (slots_b[phase, 0] + slots_b[phase, 1]) + (slots_b[phase, 2] + slots_b[phase, 3])

    def at_z(z):
        return device(x, z * 4 + ys[0], core)

    slots_b[0, zs[0]] = own[:, tail(zs[0]), :]
    tails_z = start_all(tail_copies(0, zs, lambda z: own.at[:, tail(z)], slots_b.at[0, zs[0]], at_z))
    scatter(OTHERS)
    slots_b[1, x] = sum_tails(0, tails_z)
    part_x = slots_b.at[1, x]
    tails_x = start_all(tail_copies(1, xs, lambda _: part_x, part_x, lambda to: device(to, plane, core)))
    slots_b[2, ys[0]] = sum_tails(1, tails_x)
    part_y = slots_b.at[2, ys[0]]
    tails_y = start_all(tail_copies(2, ys, lambda _: part_y, part_y, lambda y: device(x, zs[0] * 4 + y, core)))

    def spread_out(part):
        for dx, dz, dy in OTHERS:
            pltpu.make_async_remote_copy(
                src_ref=part, dst_ref=part, send_sem=ag_send, recv_sem=ag_recv.at[x],
                device_id=device(xs[dx], zs[dz] * 4 + ys[dy], core), device_id_type=MESH).start()

    def drain(part, sem):
        pltpu.make_async_copy(part, part, sem).wait()

    @pl.when(jnp.logical_not(idle))
    def _():
        tile, rows = block(which)
        slots_a[chip] = own[tile, rows, :]
        drain(slots_a.at[0:63], rs_recv)
        right[core, tile, rows, :] = jnp.sum(slots_a[...], axis=0) * 0.25
        spread_out(right.at[core, tile, rows])

    right[core, :, tail(zs[0]), :] = sum_tails(2, tails_y) * 0.25
    part_z = right.at[core, :, tail(zs[0])]
    tails_end = start_all(tail_copies(3, zs, lambda _: part_z, part_z, at_z))

    forwards = []

    def forward(rows):
        part = right.at[core, :, rows]
        copy = pltpu.make_async_remote_copy(
            src_ref=part, dst_ref=part, send_sem=half_send.at[len(forwards)], recv_sem=half_recv.at[len(forwards)],
            device_id=device(x, plane, 1 - core), device_id_type=MESH)
        copy.start()
        forwards.append(copy)

    for d in (0, 1, 3, 2):
        from_x = xs[d]
        if d == 0:

            @pl.when(idle)
            def _():
                drain(slots_a.at[0:15], ag_recv.at[x])

            @pl.when(jnp.logical_not(idle))
            def _():
                drain(slots_a.at[0:14], ag_recv.at[x])
        else:
            drain(slots_a.at[0:15], ag_recv.at[from_x])
        forward(pl.ds(pl.multiple_of(80 * from_x, 16), 80))

    for copy in tails_end:
        copy.wait_recv()
    forward(pl.ds(AD_LEFT, RANK))
    for copy in share_n:
        copy.wait_recv()
    norm_out[...] = norm_slots[0] + norm_slots[1] + norm_slots[2] + norm_slots[3]
    for copy in forwards:
        copy.wait_recv()
    for copy in share_a + share_b + share_n + [swap_a, swap_b] + tails_z + tails_x + tails_y + tails_end + forwards:
        copy.wait_send()

    @pl.when(idle)
    def _():
        drain(slots_a.at[0:60], rs_send)

    @pl.when(jnp.logical_not(idle))
    def _():
        drain(slots_a.at[0:59], rs_send)
        drain(slots_a.at[0:63], ag_send)

    for copy in loads[8:]:
        copy.wait()

def invert(gram):
    lane = lax.broadcasted_iota(jnp.int32, (8, 128), 1)
    column = lane % RANK
    base = lane - column
    sub = lax.broadcasted_iota(jnp.int32, (8, 128), 0)
    a = [[gram[8 * g : 8 * g + 8, 128 * l : 128 * l + 128] for l in range(3)] for g in range(4)]
    picks = [[jnp.take_along_axis(a[g][l], base, axis=1) for g in range(4)] for l in range(3)]
    for p in range(RANK):
        gp, sp = p // 8, p % 8
        for l in range(3):
            pick = picks[l]
            pivot = pick[0][sp : sp + 1, :]
            if p + 1 < RANK:
                ahead = [jnp.take_along_axis(a[g][l], base + p + 1, axis=1) for g in range(gp, 4)]
                ratio = ahead[0][sp : sp + 1, :] / pivot
                ahead = [c - f * ratio for c, f in zip(ahead, pick)]
                picks[l] = ahead[(p + 1) // 8 - gp :]
            row = jnp.where(column[:1] == p, 1.0, a[gp][l][sp : sp + 1, :]) / pivot
            for g in range(gp, 4):
                f = pick[g - gp]
                keep = jnp.where(column == p, 0.0, a[g][l])
                new = keep - f * row
                a[g][l] = jnp.where(sub > sp, new, a[g][l]) if g == gp else new
    out = []
    for g in range(4):
        parts = []
        for l in range(3):
            i = sub + 8 * g
            pivot = jnp.take_along_axis(a[g][l], base + i, axis=1)
            value = jnp.where(column < i, a[g][l], jnp.where(column == i, 1.0, 0.0))
            parts.append(value / jnp.sqrt(pivot))
        out.append(jnp.concatenate(parts, 1))
    return jnp.concatenate(out, 0)


def finish_kernel(
    merged, aw, dw, ew, am, dm, em, warm, right, left, norm_total, norm_scale, norm_momentum,
    au_hbm, du_hbm, eu_hbm, ac_hbm, dc_hbm, ec_hbm, ar_hbm, dr_hbm, er_hbm, av_hbm, dv_hbm, ev_hbm,
    next_hbm, norm_updated, norm_velocity,
    au, du, eu, ac, dc, ec, ar, dr, er, av, dv, ev, start, wide, out_sem,
):
    velocity = 0.9 * norm_momentum[...] + norm_total[0:3, 0:24] / 4
    norm_velocity[...] = velocity
    norm_updated[...] = norm_scale[...] - 0.05 * velocity

    wide[LEFT:, :] = jnp.zeros((32, D), F32)
    wide[0:LEFT, :] = warm[...].reshape(LEFT, D)
    factor = jnp.concatenate([right[h, t] for h in range(2) for t in range(TILES)], 1)
    gram = exact(factor, wide[...], NT)
    mi = lax.broadcasted_iota(jnp.int32, (LEFT, HALF), 0) // RANK
    mj = lax.broadcasted_iota(jnp.int32, (LEFT, HALF), 1) // RANK
    same = mi == mj
    gram = fold(jnp.where(same, gram, 0.0), NMAT)
    i = lax.broadcasted_iota(jnp.int32, (RANK, HALF), 0)
    j = lax.broadcasted_iota(jnp.int32, (RANK, HALF), 1)
    gram = jnp.where(j < LEFT, gram, jnp.where(i == j - LEFT, 1.0, 0.0))
    inverse = invert(gram)
    inverse = jnp.where(same, jnp.concatenate([inverse] * NMAT, 0), 0.0)[:, 0:LEFT]
    start[...] = exact(inverse, factor, NN)
    copies = []

    def send(src, dst):
        copy = pltpu.make_async_copy(src, dst, out_sem.at[len(copies)])
        copy.start()
        copies.append(copy)

    send(start, next_hbm)
    spread = jnp.where(row_mask(LEFT, ROWS), jnp.concatenate([left[...]] * NMAT, 0), 0.0)
    ortho = exact(inverse, spread, NN)
    oh, ol = split(ortho)
    oh, ol = oh.T, ol.T
    sh, sl = split(start[...])

    def approx(row, rows):
        part = slice(row, row + rows)
        return dot3((oh[part], ol[part]), (sh, sl), NN)

    def write(value, row, rows, w, m, u, c, r, v):
        r[...] = merged[row : row + rows, :] - value
        velocity = 0.9 * m[...] + value
        updated = w[...] - 0.05 * velocity
        v[...] = velocity
        u[...] = updated
        c[...] = updated.astype(BF16)

    for m in range(0, 8, 4):
        value = approx(24 * m, 96)
        for k in range(4):
            write(value[24 * k : 24 * k + 24], 24 * (m + k), 24, aw.at[m + k], am.at[m + k],
                  au.at[m + k], ac.at[m + k], ar.at[0, m + k], av.at[m + k])
        part = pl.ds(m, 4)
        for a, b in ((au, au_hbm), (ac, ac_hbm), (av, av_hbm)):
            send(a.at[part], b.at[part])
        send(ar.at[0, part], ar_hbm.at[0, part])
    for m in range(2):
        write(approx(192 + 96 * m, 96), 192 + 96 * m, 96, dw.at[m], dm.at[m],
              du.at[m], dc.at[m], dr.at[0, m], dv.at[m])
    for a, b in ((du, du_hbm), (dc, dc_hbm), (dr, dr_hbm), (dv, dv_hbm)):
        send(a, b)
    for m in range(2):
        part = pl.ds(128 * m, 128)
        write(approx(AD_ROWS + 128 * m, 128), AD_ROWS + 128 * m, 128, ew.at[part], em.at[part],
              eu.at[part], ec.at[part], er.at[0, part], ev.at[part])
        for a, b in ((eu, eu_hbm), (ec, ec_hbm), (ev, ev_hbm)):
            send(a.at[part], b.at[part])
        send(er.at[0, part], er_hbm.at[0, part])
    for copy in copies:
        copy.wait()


ANY = pl.BlockSpec(memory_space=pl.ANY)
VMEM = pl.BlockSpec(memory_space=pltpu.VMEM)
DMA = pltpu.SemaphoreType.DMA


def body(
    attention_grad, dense_grad, embedding_grad, attention_error, dense_error, embedding_error,
    attention_weight, dense_weight, embedding_weight, attention_momentum, dense_momentum, embedding_momentum,
    warm_start, norm_scale, norm_momentum, norm_grad,
):
    def pin(*arrays):
        return [pltpu.with_memory_space_constraint(a, pltpu.HBM) for a in arrays]

    grads = pin(attention_grad, dense_grad, embedding_grad)
    errors = pin(attention_error, dense_error, embedding_error)
    weights = pin(attention_weight, dense_weight, embedding_weight)
    momenta = pin(attention_momentum, dense_momentum, embedding_momentum)
    state = weights + momenta

    def like(arrays, dtype=None):
        return [pltpu.VMEM(a.shape, dtype or a.dtype) for a in arrays]

    def shape(a, dtype=None):
        return jax.ShapeDtypeStruct(a.shape, dtype or a.dtype)

    right, left, norm_total, merged, warm, *state = pl.pallas_call(
        exchange_kernel,
        name="exchange",
        out_shape=(
            jax.ShapeDtypeStruct((2, TILES, LEFT, 128), F32),
            jax.ShapeDtypeStruct((RANK, ROWS), F32),
            jax.ShapeDtypeStruct((8, 128), F32),
            jax.ShapeDtypeStruct((ROWS, D), F32),
            shape(warm_start),
            *[shape(a) for a in state],
        ),
        in_specs=[ANY] * 14,
        out_specs=(VMEM,) * 11,
        scratch_shapes=like(grads) + like(errors) + [
            pltpu.VMEM((3, 1, 24), F32),
            pltpu.VMEM((2, ROWS, HALF), BF16),
            pltpu.VMEM((2, ROWS, HALF), BF16),
            pltpu.VMEM((4, RANK, AD_ROWS), F32),
            pltpu.VMEM((4, RANK, 256), F32),
            pltpu.VMEM((TILES, LEFT, 128), F32),
            pltpu.VMEM((TILES, LEFT, 128), F32),
            pltpu.VMEM((TILES, LEFT, 128), F32),
            pltpu.VMEM((64, 16, 128), F32),
            pltpu.VMEM((3, 4, TILES, 8, 128), F32),
            pltpu.VMEM((4, 8, 128), F32),
            DMA((14,)), DMA((2, 3)), DMA((2, 3)), DMA((2,)), DMA((2,)), DMA, DMA,
            DMA, DMA((4,)), DMA((4, 3)), DMA((4, 3)), DMA((5,)), DMA((5,)), DMA((3,)), DMA((3,)),
        ],
        compiler_params=pltpu.CompilerParams(collective_id=0, has_side_effects=True, vmem_limit_bytes=20 << 20),
    )(*grads, *errors, *pin(warm_start, jnp.transpose(norm_grad, (1, 0, 2))), *state)

    shapes = [
        *[jax.ShapeDtypeStruct(a.shape, F32) for a in weights],
        *[jax.ShapeDtypeStruct(a.shape, BF16) for a in weights],
        *[jax.ShapeDtypeStruct(a.shape, F32) for a in errors],
        *[jax.ShapeDtypeStruct(a.shape, F32) for a in weights],
        jax.ShapeDtypeStruct((LEFT, D), F32),
        jax.ShapeDtypeStruct(norm_scale.shape, F32),
        jax.ShapeDtypeStruct(norm_scale.shape, F32),
    ]
    outs = pl.pallas_call(
        finish_kernel,
        name="finish",
        out_shape=tuple(shapes),
        in_specs=[VMEM] * 13,
        out_specs=tuple([ANY] * 13 + [VMEM] * 2),
        scratch_shapes=like(weights) + like(weights, BF16) + like(errors) + like(weights) + [
            pltpu.VMEM((LEFT, D), F32), pltpu.VMEM((HALF, D), F32), DMA((21,)),
        ],
        compiler_params=pltpu.CompilerParams(vmem_limit_bytes=24 << 20),
    )(merged, *state, warm, right, left, norm_total, norm_scale, norm_momentum)
    outs = list(outs)
    outs[12] = outs[12].reshape(NMAT, RANK, D)
    return tuple(outs)


def solution(mesh):
    matrices = (P(None, "shard", None), P(None, "shard", None), P("shard", None))
    replicas = (P("rep", None, "shard", None), P("rep", None, "shard", None), P("rep", "shard", None))
    norm = P(None, "shard")
    return jax.shard_map(
        body,
        mesh=mesh,
        in_specs=replicas + replicas + matrices + matrices + (P(), norm, norm, P("rep", None, "shard")),
        out_specs=matrices + matrices + replicas + matrices + (P(), norm, norm),
        check_vma=False,
    )
```
